32 devices in a mesh: req: 8 (over z, x), mlp: 4 (over y, core).
Axes of the slice: x: 2, y: 2, z: 4, core: 2. Of those that a mesh axis runs over, the one named last changes fastest.
Arguments:
- tokens: bfloat16 [8192, 2048], P('req'), may hold values from -6 to 6
- first_gain: float32 [2048], replicated, may hold values from 0.5 to 1.5
- joined_weight: bfloat16 [2048, 6144], P(None, 'mlp'), may hold values from -0.125 to 0.125
- dense_weight: bfloat16 [2048, 2048], P('mlp'), may hold values from -0.125 to 0.125
- adapter_down: bfloat16 [64, 16, 2048], P('req', None, 'mlp'), may hold values from -0.125 to 0.125
- adapter_up: bfloat16 [64, 16, 2048], P('req'), may hold values from -1.5 to 1.5
- adapter_ids: int32 [64], replicated, may hold values from 0 to 63, as said below
- adapter_rows: int32 [64], replicated, may hold values from 0 to 63, each once
- second_gain: float32 [2048], replicated, may hold values from 0.5 to 1.5
- up_weight: bfloat16 [2048, 8192], P(None, 'mlp'), may hold values from -0.125 to 0.125
- down_weight: bfloat16 [8192, 2048], P('mlp'), may hold values from -0.0625 to 0.0625
- page_pool: bfloat16 [96, 128, 4096], P('req', None, 'mlp'), may hold values from -100 to 100
- page_table: int32 [16, 4], P('req'), may hold values from 0 to 11, as said below
- group_index: int32 [64], P('req'), may hold values from 0 to 1
- lengths: int32 [64], P('req'), may hold values from 1 to 128, as said below
- migrants: int32 [32], P('req'), may hold values from 0 to 7, as said below
- landing: int32 [32], replicated, may hold values from 0 to 63, as said below
Outputs:
- layer_out: bfloat16 [8192, 2048], P(('req', 'mlp'))
- page_out: bfloat16 [64, 128, 4096], P('req', None, 'mlp')
The draws below stay inside these ranges and needn't reach their ends.
Inputs may be any that keep to these rules, and one draw needn't show every extreme that they name: `adapter_ids`: the requests name exactly 16 distinct adapters in all. `lengths`: each request owner holds at least one request of 128 tokens. `page_table`: the 8 entries of one owner's rows are distinct. `migrants`: entries m // 4 = o name 4 distinct requests of owner o. `landing`: A rearrangement of the slots (m // 4) * 8 + migrants[m] of all migrating requests; the 4 requests of one owner land on 4 distinct other owners, and every owner receives exactly 4 of them.
All inputs are finite; a program needn't handle non-finite values.
Results may differ from the reference program's by a relative error of at most 0.013.
The reference program's roundings to bfloat16 on the way count: a program that leaves them out, or rounds other values in their place, can miss the bound.
Values may be sent and summed in bfloat16 or wider, within the bound.
A program may use at most 192 MiB of HBM per device.

```python
import math
import jax
import jax.numpy as jnp
from jax import lax

D = 2048
HEADS = 16
HD = 128
FF = 8192
RANK = 16
ADAPTERS = 64
ACTIVE = 16
RQ_DEV = 8
SLOT = 128
PAGE = 128
PREF_PAGES = 4
GROUPS_DEV = 2
POOL_DEV = 12
MIG_DEV = 4
REQS = 64
TOKENS = 8192
N_REQ = 8
N_MLP = 4


def draw_page_pool(key, part):
    shape = (N_REQ * POOL_DEV, PAGE, 2 * D)
    first = jax.random.fold_in(key, 0)
    return jnp.clip(jax.random.normal(first, shape, jnp.float32), -6.0, 6.0).astype(jnp.bfloat16)


def draw_page_table(key, part):
    owner_keys = jax.random.split(key, N_REQ)
    orders = jax.vmap(lambda one: jax.random.permutation(one, POOL_DEV))(owner_keys)
    return orders[:, :GROUPS_DEV * PREF_PAGES].reshape(N_REQ * GROUPS_DEV, PREF_PAGES).astype(jnp.int32)


def draw_lengths(key, part):
    first, second, third = jax.random.split(key, 3)
    limit = jax.random.randint(first, (N_REQ, 1), SLOT // 4, SLOT + 1)
    lowest = jnp.maximum(limit // 2, 1)
    values = jax.random.randint(second, (N_REQ, RQ_DEV), lowest, limit + 1)
    longest = jax.random.randint(third, (N_REQ, 1), 0, RQ_DEV)
    values = jnp.where(jnp.arange(RQ_DEV)[None, :] == longest, SLOT, values)
    return values.reshape(-1).astype(jnp.int32)


def draw_adapter_ids(key, part):
    first, second, third = jax.random.split(key, 3)
    active_set = jax.random.permutation(first, ADAPTERS)[:ACTIVE]
    picked_rank = jax.random.randint(second, (REQS,), 0, ACTIVE)
    order = jax.random.permutation(third, REQS)
    picked_rank = picked_rank.at[order[:ACTIVE]].set(jnp.arange(ACTIVE))
    return active_set[picked_rank].astype(jnp.int32)


def migration_plan(key):
    base = jax.random.fold_in(key, 7)
    first, second, third, fourth = jax.random.split(base, 4)
    owner_keys = jax.random.split(first, N_REQ)
    orders = jax.vmap(lambda one: jax.random.permutation(one, RQ_DEV))(owner_keys)[:, :MIG_DEV]
    relabel = jax.random.permutation(second, N_REQ).astype(jnp.int32)
    inverse = jnp.argsort(relabel).astype(jnp.int32)
    shifts = (1 + jax.random.permutation(third, N_REQ - 1)[:MIG_DEV]).astype(jnp.int32)
    dest = inverse[(relabel[:, None] + shifts[None, :]) % N_REQ]
    slot_keys = jax.random.split(fourth, N_REQ)
    slot_orders = jax.vmap(lambda one: jax.random.permutation(one, MIG_DEV))(slot_keys).astype(jnp.int32)
    column = jnp.arange(MIG_DEV, dtype=jnp.int32)[None, :]
    picked = slot_orders[dest, jnp.broadcast_to(column, dest.shape)]
    targets = dest * RQ_DEV + orders[dest, picked]
    return (orders.reshape(-1), targets.reshape(-1))


def draw_migrants(key, part):
    return migration_plan(key)[0].astype(jnp.int32)


def draw_landing(key, part):
    return migration_plan(key)[1].astype(jnp.int32)


def with_ends(drawn, own_key, smallest, high):
    spot = [jax.random.randint(jax.random.fold_in(own_key, axis), (), 0, length) for axis, length in enumerate(drawn.shape)]
    main_axis = drawn.shape.index(max(drawn.shape))
    next_to = spot[:main_axis] + [(spot[main_axis] + 1) % drawn.shape[main_axis]] + spot[main_axis + 1:]
    return drawn.at[tuple(spot)].set(smallest).at[tuple(next_to)].set(high)


def levels(stream_key, dims, cuts, least, top_value):
    factor_of, own = 1.0, jax.random.fold_in(stream_key, 6)
    for position, parts in cuts:
        steps = jnp.exp(jax.random.uniform(jax.random.fold_in(own, position), (parts,), jnp.float32, least / len(cuts), top_value / len(cuts)))
        factor_of = factor_of * jnp.repeat(steps, dims[position] // parts).reshape([-1 if axis == position else 1 for axis in range(len(dims))])
    return factor_of


def bell_draw(stream_key, extent, spread, most, pieces=(), kind=jnp.bfloat16):
    array = spread * jax.random.normal(stream_key, extent, jnp.float32)
    if pieces:
        array = array * levels(stream_key, extent, pieces, -0.22, 0.18)
    return jnp.clip(array, -most, most).astype(kind)


def setup_inputs(seed: int = 0) -> dict:
    key_of = jax.random.split(jax.random.key(seed), 18)
    tokens = bell_draw(key_of[0], (TOKENS, D), 1.0, 6.0, ((0, 8),))
    first_gain = jnp.clip(1.0 + 0.1 * jax.random.normal(key_of[1], (D,), jnp.float32), 0.5, 1.5)
    joined_weight = bell_draw(key_of[2], (D, 3 * D), D ** -0.5, 0.125, ((1, 4),))
    dense_weight = bell_draw(key_of[3], (D, D), D ** -0.5, 0.125, ((0, 4),))
    adapter_down = bell_draw(key_of[4], (ADAPTERS, RANK, D), D ** -0.5, 0.125, ((0, 8), (2, 4)))
    adapter_up = bell_draw(key_of[5], (ADAPTERS, RANK, D), RANK ** -0.5, 1.5, ((0, 8),))
    adapter_ids = draw_adapter_ids(jax.random.fold_in(key_of[17], 71), 0)
    adapter_rows = jax.random.permutation(key_of[7], ADAPTERS).astype(jnp.int32)
    second_gain = jnp.clip(1.0 + 0.1 * jax.random.normal(key_of[8], (D,), jnp.float32), 0.5, 1.5)
    up_weight = bell_draw(key_of[9], (D, FF), D ** -0.5, 0.125, ((1, 4),))
    down_weight = bell_draw(key_of[10], (FF, D), FF ** -0.5, 0.0625, ((0, 4),))
    page_pool = draw_page_pool(jax.random.fold_in(key_of[17], 71), 0)
    page_table = draw_page_table(jax.random.fold_in(key_of[17], 71), 0)
    group_index = with_ends(jax.random.randint(key_of[13], (REQS,), 0, GROUPS_DEV), jax.random.fold_in(key_of[13], 1), 0, GROUPS_DEV - 1).astype(jnp.int32)
    lengths = draw_lengths(jax.random.fold_in(key_of[17], 71), 0)
    migrants = draw_migrants(jax.random.fold_in(key_of[17], 71), 0)
    landing = draw_landing(jax.random.fold_in(key_of[17], 71), 0)
    return {"tokens": tokens, "first_gain": first_gain, "joined_weight": joined_weight, "dense_weight": dense_weight, "adapter_down": adapter_down, "adapter_up": adapter_up, "adapter_ids": adapter_ids, "adapter_rows": adapter_rows, "second_gain": second_gain, "up_weight": up_weight, "down_weight": down_weight, "page_pool": page_pool, "page_table": page_table, "group_index": group_index, "lengths": lengths, "migrants": migrants, "landing": landing}


EPS = 1e-05

def layer_norm(values, gain):
    values = values.astype(jnp.float32)
    mean = lax.optimization_barrier(jnp.mean(values, axis=-1, keepdims=True))
    centred = values - mean
    variance = lax.optimization_barrier(jnp.mean(centred * centred, axis=-1, keepdims=True))
    return (centred * lax.rsqrt(variance + EPS) * gain.astype(jnp.float32)).astype(jnp.bfloat16)

def gelu_tanh(value):
    return 0.5 * value * (1.0 + jnp.tanh(0.7978845608 * (value + 0.044715 * value * value * value)))

def rounded(value):
    return lax.optimization_barrier(value.astype(jnp.bfloat16)).astype(jnp.float32)

def attend(queries, keys, values, prefix_keys, prefix_values, lens, slopes):
    scale = 1.0 / math.sqrt(queries.shape[-1])
    own_len = queries.shape[1]
    pre_len = prefix_keys.shape[1]
    query_f = queries.astype(jnp.float32)
    s_pre = jnp.einsum('rihe,rphe->rhip', query_f, prefix_keys.astype(jnp.float32)) * scale
    s_own = jnp.einsum('rihe,rjhe->rhij', query_f, keys.astype(jnp.float32)) * scale
    own_pos = jnp.arange(own_len).astype(jnp.float32)
    pre_pos = jnp.arange(pre_len).astype(jnp.float32)
    s_pre = s_pre - slopes[None, :, None, None] * ((pre_len + own_pos)[:, None] - pre_pos[None, :])[None, None]
    s_own = s_own - slopes[None, :, None, None] * (own_pos[:, None] - own_pos[None, :])[None, None]
    steps = jnp.arange(own_len, dtype=jnp.int32)
    allowed = (steps[None, :] <= steps[:, None])[None, None] & (steps[None, None, None, :] < lens[:, None, None, None])
    s_own = jnp.where(allowed, s_own, -jnp.inf)
    top = jnp.maximum(lax.optimization_barrier(jnp.max(s_pre, axis=-1)), lax.optimization_barrier(jnp.max(s_own, axis=-1)))[..., None]
    e_pre = jnp.exp(s_pre - top)
    e_own = jnp.exp(s_own - top)
    total = lax.optimization_barrier(jnp.sum(e_pre, axis=-1, keepdims=True)) + lax.optimization_barrier(jnp.sum(e_own, axis=-1, keepdims=True))
    w_pre = (e_pre / total).astype(jnp.bfloat16)
    w_own = (e_own / total).astype(jnp.bfloat16)
    mixed = jnp.einsum('rhip,rphe->rihe', w_pre.astype(jnp.float32), prefix_values.astype(jnp.float32))
    mixed = mixed + jnp.einsum('rhij,rjhe->rihe', w_own.astype(jnp.float32), values.astype(jnp.float32))
    return mixed.astype(jnp.bfloat16)

def reference(tokens, first_gain, joined_weight, dense_weight, adapter_down, adapter_up, adapter_ids, adapter_rows, second_gain, up_weight, down_weight, page_pool, page_table, group_index, lengths, migrants, landing):
    row_count = RQ_DEV * SLOT
    block = D // N_MLP
    hidden_block = FF // N_MLP
    head_pos = jnp.arange(HEADS).astype(jnp.float32)
    slopes = jnp.exp2(-8.0 * (head_pos + 1.0) / HEADS)
    table_rows = adapter_rows[adapter_ids]
    chosen_down = adapter_down[table_rows]
    chosen_up = adapter_up[table_rows]

    def one_owner(inputs):
        block_tokens, down_sel, up_sel, pool, table, groups, lens = inputs
        normed = layer_norm(block_tokens, first_gain)
        joined = jnp.dot(normed, joined_weight, preferred_element_type=jnp.float32).astype(jnp.bfloat16)
        joined = joined.reshape(RQ_DEV, SLOT, HEADS, 3, HD)
        valid = jnp.arange(SLOT, dtype=jnp.int32)[None, :] < lens[:, None]
        fresh = joined[:, :, :, 1:, :].reshape(RQ_DEV, SLOT, 2 * D)
        fresh = jnp.where(valid[:, :, None], fresh, jnp.zeros((), jnp.bfloat16))
        pages = table[groups]
        prefix = pool.reshape(POOL_DEV, PAGE, HEADS, 2, HD)[pages]
        prefix = prefix.reshape(RQ_DEV, PREF_PAGES * PAGE, HEADS, 2, HD)
        attended = attend(joined[:, :, :, 0], joined[:, :, :, 1], joined[:, :, :, 2], prefix[:, :, :, 0], prefix[:, :, :, 1], lens, slopes)
        attended_rows = attended.reshape(row_count, D)
        attended_req = attended.reshape(RQ_DEV, SLOT, D)
        dense = jnp.zeros((row_count, D), jnp.float32)
        low = jnp.zeros((RQ_DEV, SLOT, RANK), jnp.float32)
        for index in range(N_MLP):
            lo_col = index * block
            dense = dense + rounded(jnp.dot(attended_rows[:, lo_col:lo_col + block], dense_weight[lo_col:lo_col + block], preferred_element_type=jnp.float32))
            low = low + rounded(jnp.einsum('rsd,rkd->rsk', attended_req[:, :, lo_col:lo_col + block].astype(jnp.float32), down_sel[:, :, lo_col:lo_col + block].astype(jnp.float32)))
        low = low.astype(jnp.bfloat16)
        delta = jnp.einsum('rsk,rkd->rsd', low.astype(jnp.float32), up_sel.astype(jnp.float32)).reshape(row_count, D)
        residual = (block_tokens.astype(jnp.float32) + dense + delta).astype(jnp.bfloat16)
        normed_two = layer_norm(residual, second_gain)
        expanded = gelu_tanh(jnp.dot(normed_two, up_weight, preferred_element_type=jnp.float32)).astype(jnp.bfloat16)
        feed = jnp.zeros((row_count, D), jnp.float32)
        for index in range(N_MLP):
            lo_unit = index * hidden_block
            feed = feed + rounded(jnp.dot(expanded[:, lo_unit:lo_unit + hidden_block], down_weight[lo_unit:lo_unit + hidden_block], preferred_element_type=jnp.float32))
        result = jnp.where(valid.reshape(row_count)[:, None], residual.astype(jnp.float32) + feed, jnp.zeros((), jnp.float32))
        return (result.astype(jnp.bfloat16), fresh)
    outputs, fresh_all = lax.map(one_owner, (tokens.reshape(N_REQ, row_count, D), chosen_down.reshape(N_REQ, RQ_DEV, RANK, D), chosen_up.reshape(N_REQ, RQ_DEV, RANK, D), page_pool.reshape(N_REQ, POOL_DEV, PAGE, 2 * D), page_table.reshape(N_REQ, GROUPS_DEV, PREF_PAGES), group_index.reshape(N_REQ, RQ_DEV), lengths.reshape(N_REQ, RQ_DEV)))
    layer_out = outputs.reshape(TOKENS, D)
    fresh_all = fresh_all.reshape(REQS, SLOT, 2 * D)
    sources = jnp.arange(N_REQ * MIG_DEV, dtype=jnp.int32) // MIG_DEV * RQ_DEV + migrants.astype(jnp.int32)
    anchor = jnp.arange(REQS, dtype=jnp.int32).at[landing.astype(jnp.int32)].set(sources)
    page_out = fresh_all[anchor]
    return (layer_out, page_out)
```

```python
import functools
import math

import jax
import jax.numpy as jnp
from jax import lax
from jax.experimental import pallas as pl
from jax.experimental.pallas import tpu as pltpu
from jax.sharding import PartitionSpec as P

HEADS = 16
HD = 128
EPS = 1e-05
LOG2E = 1.4426950408889634
MESH = pl.DeviceIdType.MESH
F32 = jnp.float32
BF16 = jnp.bfloat16


def layer_norm(values, gain):
    mean = jnp.mean(values, axis=-1, keepdims=True)
    centred = values - mean
    variance = jnp.mean(centred * centred, axis=-1, keepdims=True)
    return (centred * lax.rsqrt(variance + EPS) * gain).astype(BF16)


def gelu_tanh(value):
    return 0.5 * value * (1.0 + jnp.tanh(0.7978845608 * (value + 0.044715 * value * value * value)))


def body(
    n_req,
    n_mlp,
    ids,
    id_rows,
    table,
    groups,
    lens,
    migrants,
    landing,
    gain_one,
    gain_two,
    tokens,
    joined_w,
    dense_w,
    adown,
    aup,
    up_w,
    down_w,
    pool,
    layer_out,
    page_out,
    w_one,
    w_up,
    w_dense,
    pool_v,
    tok,
    joined,
    dist,
    att,
    part,
    part_in,
    pair_own,
    pair_in,
    fresh,
    mig_out,
    mig_in,
    res,
    normed,
    expanded,
    feed,
    feed_in,
    pair_feed,
    final_in,
    out_v,
    tab,
    sel_out,
    sel_in,
    down_rows,
    up_out,
    up_rows,
    low_out,
    low_in,
    load_sem,
    tok_sem,
    res_sem,
    out_sem,
    page_sem,
    part_s,
    part_r,
    pair_s,
    pair_r,
    mig_s,
    mig_r,
    norm_s,
    norm_r,
    feed_s,
    feed_r,
    final_s,
    final_r,
    tab_s,
    tab_r,
    sel_s,
    sel_r,
    uprow_s,
    uprow_r,
    low_s,
    low_r,
):
    r = lax.axis_index("req")
    m = lax.axis_index("mlp")
    chips = n_mlp // 2
    y = m // 2
    c = m % 2
    lines = n_req // chips
    z = r // chips
    x = r % chips
    nq = lens.shape[0]
    slot = tokens.shape[0] // nq
    width = tokens.shape[1]
    jw = joined_w.shape[1]
    heads = jw // (3 * HD)
    cols = heads * HD
    own = nq // n_mlp
    chunks = chips * own
    moves = migrants.shape[0]
    n_pages = table.shape[1]
    page = pool_v.shape[1]
    pre = n_pages * page
    total = pre + slot
    rank = adown.shape[1]
    rows_per = adown.shape[0]
    hidden = up_w.shape[1]
    partner = m + 1 - 2 * c

    def peer(jj):
        return lax.rem(m + jj, n_mlp)

    def remote(src, dst, s, d, to_r, to_m):
        return pltpu.make_async_remote_copy(
            src_ref=src, dst_ref=dst, send_sem=s, recv_sem=d, device_id=(to_r, to_m), device_id_type=MESH
        )

    loads = {
        "pool": pltpu.make_async_copy(pool, pool_v, load_sem.at[0]),
        "joined": pltpu.make_async_copy(joined_w, w_one.at[pl.ds(0, width), pl.ds(0, jw)], load_sem.at[1]),
        "dense": pltpu.make_async_copy(dense_w, w_dense, load_sem.at[2]),
        "up": pltpu.make_async_copy(up_w, w_up, load_sem.at[3]),
        "down": pltpu.make_async_copy(down_w, w_one.at[pl.ds(0, hidden), pl.ds(0, width)], load_sem.at[4]),
        "adown": pltpu.make_async_copy(adown, tab.at[z, :, pl.ds(0, rank), :], load_sem.at[5]),
        "aup": pltpu.make_async_copy(
            aup.at[:, :, pl.ds(pl.multiple_of(m * cols, 128), cols)],
            tab.at[z, :, pl.ds(rank, rank), :],
            load_sem.at[6],
        ),
    }

    def first_chip(t):
        return lax.rem(y + t // own, chips)

    def request(chip, core, s):
        return chip * (2 * own) + core * own + s

    def tok_copy(t, h):
        q = request(first_chip(t), h, t % own)
        return pltpu.make_async_copy(
            tokens.at[pl.ds(pl.multiple_of(q * slot, slot), slot)],
            tok.at[t % 2, pl.ds(h * slot, slot)],
            tok_sem.at[t % 2, h],
        )

    for h in range(2):
        tok_copy(0, h).start()
    loads["joined"].start()
    loads["adown"].start()
    loads["aup"].start()
    loads["pool"].start()
    loads["dense"].start()
    for h in range(2):
        if chunks > 1:
            tok_copy(1, h).start()
    res_loads = []
    for chip in range(chips):
        for s in range(own):
            q = request(chip, c, s)
            res_loads.append(
                pltpu.make_async_copy(
                    tokens.at[pl.ds(pl.multiple_of(q * slot, slot), slot)],
                    res.at[chip * own + s],
                    res_sem.at[chip * own + s],
                )
            )
    for d in res_loads:
        d.start()
    loads["up"].start()

    barrier = pltpu.get_barrier_semaphore()
    for k in range(1, n_req):
        pl.semaphore_signal(barrier, inc=1, device_id=(lax.rem(r + k, n_req), m), device_id_type=MESH)
    for k in range(1, n_mlp):
        pl.semaphore_signal(barrier, inc=1, device_id=(r, peer(k)), device_id_type=MESH)

    row = lax.broadcasted_iota(jnp.int32, (slot, total), 0)
    col = lax.broadcasted_iota(jnp.int32, (slot, total), 1)
    dist[...] = (pre + row - col).astype(F32)

    def norm_tokens(t):
        for h in range(2):
            tok_copy(t, h).wait()

        def one(i, carry):
            at = pl.ds(pl.multiple_of(i * 64, 64), 64)
            tok[t % 2, at] = layer_norm(tok[t % 2, at].astype(F32), gain_one[...])
            return carry

        lax.fori_loop(0, 2 * slot // 64, one, 0)

    def project(t):
        tile = min(512, jw)

        def one(i, carry):
            at = pl.ds(pl.multiple_of(i * tile, tile), tile)
            joined[:, at] = jnp.dot(
                tok[t % 2], w_one[pl.ds(0, width), at], preferred_element_type=F32
            ).astype(BF16)
            return carry

        lax.fori_loop(0, jw // tile, one, 0)

    def attend(t, h):
        q = request(first_chip(t), h, t % own)
        length = lens[q]
        g = groups[q]
        rows = pl.ds(h * slot, slot)
        own_row = lax.broadcasted_iota(jnp.int32, (slot, slot), 0)
        own_col = lax.broadcasted_iota(jnp.int32, (slot, slot), 1)
        allowed = (own_col <= own_row) & (own_col < length)
        valid = lax.broadcasted_iota(jnp.int32, (slot, 2 * HD), 0) < length
        pages = [table[g, p] for p in range(n_pages)]
        for k in range(heads):
            slope = jnp.float32(0.0)
            for i in range(n_mlp):
                here = 2.0 ** (-8.0 * (i * heads + k + 1.0) / HEADS) * LOG2E
                slope = jnp.where(m == i, jnp.float32(here), slope)
            at = k * 3 * HD
            query = joined[rows, at : at + HD]
            kv = joined[rows, at + HD : at + 3 * HD]
            fresh[q, :, k * 2 * HD : (k + 1) * 2 * HD] = jnp.where(valid, kv, jnp.zeros((), BF16))
            keys = jnp.concatenate(
                [pool_v[i, :, k * 2 * HD : k * 2 * HD + HD] for i in pages] + [kv[:, :HD]], axis=0
            )
            values = jnp.concatenate(
                [pool_v[i, :, k * 2 * HD + HD : (k + 1) * 2 * HD] for i in pages] + [kv[:, HD:]], axis=0
            )
            scores = lax.dot_general(query, keys, (((1,), (1,)), ((), ())), preferred_element_type=F32)
            scores = scores * (LOG2E / math.sqrt(HD)) - slope * dist[...]
            scores = jnp.concatenate(
                [scores[:, :pre], jnp.where(allowed, scores[:, pre:], -jnp.inf)], axis=1
            )
            top = jnp.max(scores, axis=-1, keepdims=True)
            weights = jnp.exp2(scores - top)
            inverse = 1.0 / jnp.sum(weights, axis=-1, keepdims=True)
            weights = (weights * inverse).astype(BF16)
            att[t, rows, k * HD : (k + 1) * HD] = jnp.dot(
                weights, values, preferred_element_type=F32
            ).astype(BF16)

    def part_copy(t):
        theirs = pl.ds(pl.multiple_of((1 - c) * slot, slot), slot)
        return remote(part.at[t % 2, theirs], part_in.at[t % 2], part_s.at[t % 2], part_r.at[t % 2], r, partner)

    def dense(t):
        if t >= 2:
            part_copy(t - 2).wait_send()
        tile = min(512, width)

        def one(i, carry):
            at = pl.ds(pl.multiple_of(i * tile, tile), tile)
            part[t % 2, :, at] = jnp.dot(att[t], w_dense[:, at], preferred_element_type=F32).astype(BF16)
            return carry

        lax.fori_loop(0, width // tile, one, 0)

    def pair_copy(t, jy):
        at = first_chip(t) * own + t % own
        return remote(
            pair_own.at[at], pair_in.at[jy - 1, at], pair_s.at[t, jy - 1], pair_r.at[jy - 1, at], r, peer(2 * jy)
        )

    mine = pl.ds(pl.multiple_of(c * slot, slot), slot)

    def pair(t):
        part_copy(t).wait_recv()
        at = first_chip(t) * own + t % own
        pair_own[at] = (part[t % 2, mine].astype(F32) + part_in[t % 2].astype(F32)).astype(BF16)
        for jy in range(1, chips):
            pair_copy(t, jy).start()

    def line_up(step):
        at = jnp.maximum(z - step, 0)
        return (z + 1 < lines) & (z - step >= 0), remote(
            tab.at[at], tab.at[at], tab_s.at[0, step], tab_r.at[at], jnp.minimum(r + chips, n_req - 1), m
        )

    def line_down(step):
        at = jnp.minimum(z + step, lines - 1)
        return (z - 1 >= 0) & (z + step < lines), remote(
            tab.at[at], tab.at[at], tab_s.at[1, step], tab_r.at[at], jnp.maximum(r - chips, 0), m
        )

    def line_arrive(at):
        return remote(tab.at[at], tab.at[at], tab_s.at[0, 0], tab_r.at[at], r, m)

    def line_step(step):
        if step > 0:
            @pl.when(z - step >= 0)
            def _():
                line_arrive(jnp.maximum(z - step, 0)).wait_recv()

            @pl.when(z + step < lines)
            def _():
                line_arrive(jnp.minimum(z + step, lines - 1)).wait_recv()

        if step < lines - 1:
            for go, copy in (line_up(step), line_down(step)):
                @pl.when(go)
                def _(copy=copy):
                    copy.start()

    def line_end():
        for step in range(lines - 1):
            for go, copy in (line_up(step), line_down(step)):
                @pl.when(go)
                def _(copy=copy):
                    copy.wait_send()

    def table_row(request_index):
        return id_rows[ids[request_index]]

    def sel_copy(jx):
        to = z * chips + lax.rem(x + jx, chips)
        return remote(sel_out.at[jx - 1], sel_in.at[jx - 1], sel_s.at[jx - 1], sel_r.at[jx - 1], to, m)

    def select_send():
        for jx in range(1, chips):
            to = z * chips + lax.rem(x + jx, chips)
            for q in range(nq):
                t = table_row(to * nq + q)
                sel_out[jx - 1, q] = tab[(t // rows_per) // chips, t % rows_per]
            sel_copy(jx).start()

    def uprow_copy(jj):
        h = lax.rem(c + jj, 2)
        at = pl.ds(pl.multiple_of(m * cols, 128), cols)
        return remote(up_out.at[h], up_rows.at[:, :, at], uprow_s.at[jj - 1], uprow_r.at[jj - 1], r, peer(jj))

    def select_take():
        for jx in range(1, chips):
            sel_copy(jx).wait_recv()
        for chip in range(chips):
            for h in range(2):
                for s in range(own):
                    q = chip * 2 * own + h * own + s
                    t = table_row(r * nq + q)
                    o = t // rows_per
                    jx = (x - o % chips + chips) % chips
                    here = tab[o // chips, t % rows_per]
                    there = sel_in[jnp.maximum(jx - 1, 0), q]
                    both = jnp.where(jx == 0, here, there)
                    down_rows[q] = both[:rank]
                    up_out[h, chip * own + s] = both[rank:]
        for jj in range(1, n_mlp):
            uprow_copy(jj).start()
        up_rows[:, :, pl.ds(pl.multiple_of(m * cols, 128), cols)] = up_out[c]

    def low_copy(jj):
        h = lax.rem(c + jj, 2)
        return remote(low_out.at[h], low_in.at[jj - 1], low_s.at[jj - 1], low_r.at[jj - 1], r, peer(jj))

    def low_parts():
        for t in range(chunks):
            for h in range(2):
                chip = first_chip(t)
                q = request(chip, h, t % own)
                low_out[h, chip * own + t % own] = lax.dot_general(
                    down_rows[q],
                    att[t, pl.ds(h * slot, slot)],
                    (((1,), (1,)), ((), ())),
                    preferred_element_type=F32,
                ).astype(BF16)
        for jj in range(1, n_mlp):
            low_copy(jj).start()

    def mig_copy(j):
        return remote(
            mig_out.at[j - 1], mig_in.at[j - 1], mig_s.at[j - 1], mig_r.at[j - 1], lax.rem(r + j, n_req), m
        )

    def migrate():
        for j in range(1, n_req):
            to = lax.rem(r + j, n_req)
            leaving = jnp.int32(0)
            for k in range(moves):
                leaving = jnp.where(landing[r * moves + k] // nq == to, migrants[k], leaving)
            mig_out[j - 1] = fresh[leaving]
            mig_copy(j).start()

    def page_copy(s):
        return pltpu.make_async_copy(mig_out.at[s], page_out.at[s], page_sem.at[s])

    def merge():
        for j in range(1, n_req):
            mig_copy(j).wait()
        for s in range(nq):
            owner = jnp.int32(-1)
            for k in range(n_req * moves):
                owner = jnp.where(landing[k] == r * nq + s, k // moves, owner)
            at = jnp.maximum((r - owner + n_req) % n_req - 1, 0)
            mig_out[s] = jnp.where(owner >= 0, mig_in[at], fresh[s])
            page_copy(s).start()

    norm_tokens(0)
    loads["joined"].wait()
    project(0)
    loads["adown"].wait()
    loads["aup"].wait()
    pl.semaphore_wait(barrier, n_req - 1 + n_mlp - 1)
    line_step(0)
    loads["pool"].wait()
    for t in range(chunks):
        if t > 0:
            norm_tokens(t)
            project(t)
        if t + 2 < chunks:
            for h in range(2):
                tok_copy(t + 2, h).start()
        if t == chunks - 1:
            loads["down"].start()
        if t > 0:
            pair(t - 1)
        for h in range(2):
            attend(t, h)
        if t == 0:
            loads["dense"].wait()
        dense(t)
        part_copy(t).start()
        if t + 1 < lines:
            line_step(t + 1)
    for step in range(chunks + 1, lines):
        line_step(step)
    migrate()
    pair(chunks - 1)
    select_send()
    select_take()
    low_parts()
    for jj in range(1, n_mlp):
        uprow_copy(jj).wait_recv()
        low_copy(jj).wait_recv()
    loads["up"].wait()
    loads["down"].wait()
    for d in res_loads:
        d.wait()

    def second_chip(t):
        return lax.rem(y + 1 + t // own, chips)

    def norm_copy(t):
        return remote(normed.at[t, mine], normed.at[t, mine], norm_s.at[t], norm_r.at[t], r, partner)

    def residual(t):
        at = second_chip(t) * own + t % own
        for jy in range(1, chips):
            remote(
                pair_own.at[at], pair_in.at[jy - 1, at], pair_s.at[t, jy - 1], pair_r.at[jy - 1, at], r, partner
            ).wait_recv()
        low = low_out[c, at].astype(F32)
        for jj in range(1, n_mlp):
            low = low + low_in[jj - 1, at].astype(F32)
        low = low.astype(BF16)
        delta = lax.dot_general(low, up_rows[at], (((0,), (0,)), ((), ())), preferred_element_type=F32)
        value = res[at].astype(F32) + delta + pair_own[at].astype(F32)
        for jy in range(1, chips):
            value = value + pair_in[jy - 1, at].astype(F32)
        value = value.astype(BF16)
        res[at] = value
        normed[t, mine] = layer_norm(value.astype(F32), gain_two[...])
        norm_copy(t).start()

    def expand(t):
        norm_copy(t).wait_recv()
        tile = min(512, hidden)

        def one(i, carry):
            at = pl.ds(pl.multiple_of(i * tile, tile), tile)
            expanded[:, at] = gelu_tanh(
                jnp.dot(normed[t], w_up[:, at], preferred_element_type=F32)
            ).astype(BF16)
            return carry

        lax.fori_loop(0, hidden // tile, one, 0)

    def feed_copy(t):
        theirs = pl.ds(pl.multiple_of((1 - c) * slot, slot), slot)
        return remote(feed.at[t % 2, theirs], feed_in.at[t], feed_s.at[t], feed_r.at[t], r, partner)

    def contract(t):
        if t >= 2:
            feed_copy(t - 2).wait_send()
        tile = min(512, width)

        def one(i, carry):
            at = pl.ds(pl.multiple_of(i * tile, tile), tile)
            feed[t % 2, :, at] = jnp.dot(
                expanded[...], w_one[pl.ds(0, hidden), at], preferred_element_type=F32
            ).astype(BF16)
            return carry

        lax.fori_loop(0, width // tile, one, 0)
        feed_copy(t).start()

    def final_copy(t):
        jy = 1 + t // own
        s = t % own
        return remote(
            pair_feed.at[t], final_in.at[jy - 1, s], final_s.at[t], final_r.at[jy - 1, s], r, peer(2 * jy)
        )

    def gather(t):
        feed_copy(t).wait_recv()
        pair_feed[t] = (feed[t % 2, mine].astype(F32) + feed_in[t].astype(F32)).astype(BF16)
        final_copy(t).start()

    others = chunks - own
    residual(0)
    for t in range(chunks):
        expand(t)
        if 0 < t <= others:
            gather(t - 1)
        contract(t)
        if t + 1 < chunks:
            residual(t + 1)
    for t in range(max(chunks - 2, 0), chunks):
        part_copy(t).wait_send()
    for t in range(chunks):
        for jy in range(1, chips):
            pair_copy(t, jy).wait_send()
        norm_copy(t).wait_send()
    line_end()
    for jx in range(1, chips):
        sel_copy(jx).wait_send()
    for jj in range(1, n_mlp):
        uprow_copy(jj).wait_send()
        low_copy(jj).wait_send()
    merge()

    def out_copy(s):
        return pltpu.make_async_copy(out_v.at[s], layer_out.at[pl.ds(s * slot, slot)], out_sem.at[s])

    for s in range(own):
        t = others + s
        at = y * own + s
        feed_copy(t).wait_recv()
        value = res[at].astype(F32) + (feed[t % 2, mine].astype(F32) + feed_in[t].astype(F32))
        for jy in range(1, chips):
            remote(
                pair_feed.at[0], final_in.at[jy - 1, s], final_s.at[0], final_r.at[jy - 1, s], r, partner
            ).wait_recv()
            value = value + final_in[jy - 1, s].astype(F32)
        valid = lax.broadcasted_iota(jnp.int32, (slot, width), 0) < lens[m * own + s]
        out_v[s] = jnp.where(valid, value, 0.0).astype(BF16)
        out_copy(s).start()
    for t in range(others):
        final_copy(t).wait_send()
    for t in range(max(chunks - 2, 0), chunks):
        feed_copy(t).wait_send()
    for s in range(own):
        out_copy(s).wait()
    for s in range(nq):
        page_copy(s).wait()


def shards(n_req, n_mlp, *args):
    (
        tokens,
        first_gain,
        joined_weight,
        dense_weight,
        adapter_down,
        adapter_up,
        adapter_ids,
        adapter_rows,
        second_gain,
        up_weight,
        down_weight,
        page_pool,
        page_table,
        group_index,
        lengths,
        migrants,
        landing,
    ) = args
    chips = n_mlp // 2
    lines = n_req // chips
    nq = lengths.shape[0]
    slot = tokens.shape[0] // nq
    width = tokens.shape[1]
    jw = joined_weight.shape[1]
    heads = jw // (3 * HD)
    cols = heads * HD
    own = nq // n_mlp
    chunks = chips * own
    hidden = up_weight.shape[1]
    rank = adapter_down.shape[1]
    kv = page_pool.shape[2]
    total = page_table.shape[1] * page_pool.shape[1] + slot
    dma = pltpu.SemaphoreType.DMA
    vm = pltpu.VMEM
    others = max(chips - 1, 1)
    scratch = [
        vm((max(width, hidden), max(jw, width)), BF16),
        vm((width, hidden), BF16),
        vm(dense_weight.shape, BF16),
        vm(page_pool.shape, BF16),
        vm((2, 2 * slot, width), BF16),
        vm((2 * slot, jw), BF16),
        vm((slot, total), F32),
        vm((chunks, 2 * slot, cols), BF16),
        vm((2, 2 * slot, width), BF16),
        vm((2, slot, width), BF16),
        vm((chunks, slot, width), BF16),
        vm((others, chunks, slot, width), BF16),
        vm((nq, slot, kv), BF16),
        vm((max(nq, n_req - 1), slot, kv), BF16),
        vm((n_req - 1, slot, kv), BF16),
        vm((chunks, slot, width), BF16),
        vm((chunks, 2 * slot, width), BF16),
        vm((2 * slot, hidden), BF16),
        vm((2, 2 * slot, width), BF16),
        vm((chunks, slot, width), BF16),
        vm((max(chunks - own, 1), slot, width), BF16),
        vm((others, own, slot, width), BF16),
        vm((own, slot, width), BF16),
        vm((lines, adapter_down.shape[0], 2 * rank, cols), BF16),
        vm((others, nq, 2 * rank, cols), BF16),
        vm((others, nq, 2 * rank, cols), BF16),
        vm((nq, rank, cols), BF16),
        vm((2, chunks, rank, cols), BF16),
        vm((chunks, rank, width), BF16),
        vm((2, chunks, rank, slot), BF16),
        vm((n_mlp - 1, chunks, rank, slot), BF16),
        dma((7,)),
        dma((2, 2)),
        dma((chunks,)),
        dma((own,)),
        dma((nq,)),
        dma((2,)),
        dma((2,)),
        dma((chunks, others)),
        dma((others, chunks)),
        dma((n_req - 1,)),
        dma((n_req - 1,)),
        dma((chunks,)),
        dma((chunks,)),
        dma((chunks,)),
        dma((chunks,)),
        dma((chunks,)),
        dma((others, own)),
        dma((2, lines)),
        dma((lines,)),
        dma((others,)),
        dma((others,)),
        dma((n_mlp - 1,)),
        dma((n_mlp - 1,)),
        dma((n_mlp - 1,)),
        dma((n_mlp - 1,)),
    ]
    smem = pl.BlockSpec(memory_space=pltpu.SMEM)
    vmem = pl.BlockSpec(memory_space=pltpu.VMEM)
    hbm = pl.BlockSpec(memory_space=pl.ANY)
    return pl.pallas_call(
        functools.partial(body, n_req, n_mlp),
        out_shape=(
            jax.ShapeDtypeStruct((own * slot, width), BF16),
            jax.ShapeDtypeStruct((nq, slot, kv), BF16),
        ),
        in_specs=[smem] * 7 + [vmem] * 2 + [hbm] * 8,
        out_specs=(hbm, hbm),
        scratch_shapes=scratch,
        compiler_params=pltpu.CompilerParams(
            collective_id=0, has_side_effects=True, vmem_limit_bytes=63 * 1024 * 1024
        ),
    )(
        adapter_ids,
        adapter_rows,
        page_table,
        group_index,
        lengths,
        migrants,
        landing,
        first_gain.reshape(1, -1),
        second_gain.reshape(1, -1),
        tokens,
        joined_weight,
        dense_weight,
        adapter_down,
        adapter_up,
        up_weight,
        down_weight,
        page_pool,
    )


def solution(mesh):
    return jax.shard_map(
        functools.partial(shards, mesh.shape["req"], mesh.shape["mlp"]),
        mesh=mesh,
        in_specs=(
            P("req", None),
            P(),
            P(None, "mlp"),
            P("mlp", None),
            P("req", None, "mlp"),
            P("req", None, None),
            P(),
            P(),
            P(),
            P(None, "mlp"),
            P("mlp", None),
            P("req", None, "mlp"),
            P("req", None),
            P("req"),
            P("req"),
            P("req"),
            P(),
        ),
        out_specs=(P(("req", "mlp"), None), P("req", None, "mlp")),
        check_vma=False,
    )
```

```python
import functools
import math

import jax
import jax.numpy as jnp
from jax import lax
from jax.experimental import pallas as pl
from jax.experimental.pallas import tpu as pltpu
from jax.sharding import PartitionSpec as P

HEADS = 16
HD = 128
EPS = 1e-05
LOG2E = 1.4426950408889634
MESH = pl.DeviceIdType.MESH
F32 = jnp.float32
BF16 = jnp.bfloat16


def layer_norm(values, gain):
    mean = jnp.mean(values, axis=-1, keepdims=True)
    centred = values - mean
    variance = jnp.mean(centred * centred, axis=-1, keepdims=True)
    return (centred * lax.rsqrt(variance + EPS) * gain).astype(BF16)


def div(a, b):
    return a // b if isinstance(a, int) else lax.div(a, jnp.int32(b))


def rem(a, b):
    return a % b if isinstance(a, int) else lax.rem(a, jnp.int32(b))


def loop(count, step, unroll=1):
    def one(i, carry):
        step(i)
        return carry

    lax.fori_loop(0, count, one, 0, unroll=unroll)


def blocks(rows, step, unroll=2):
    loop(rows // 16, lambda i: step(i * 16 if isinstance(i, int) else pl.multiple_of(i * 16, 16)), unroll)


def gelu_tanh(value):
    return 0.5 * value * (1.0 + jnp.tanh(0.7978845608 * (value + 0.044715 * value * value * value)))


def body(
    n_req,
    n_mlp,
    ids,
    id_rows,
    table,
    groups,
    lens,
    migrants,
    landing,
    gain_one,
    gain_two,
    tokens,
    joined_w,
    dense_w,
    adown,
    aup,
    up_w,
    down_w,
    pool,
    layer_out,
    page_out,
    w_one,
    w_up,
    w_dense,
    pool_v,
    tok,
    joined,
    att,
    part,
    part_in,
    pair_own,
    pair_in,
    fresh,
    mig_out,
    mig_in,
    res,
    normed,
    expanded,
    feed,
    feed_in,
    pair_feed,
    final_in,
    out_v,
    tab,
    sel_out,
    sel_in,
    down_rows,
    up_out,
    up_rows,
    low_out,
    low_in,
    load_sem,
    tok_sem,
    res_sem,
    out_sem,
    page_sem,
    part_s,
    part_r,
    pair_s,
    pair_r,
    mig_s,
    mig_r,
    norm_s,
    norm_r,
    feed_s,
    feed_r,
    final_s,
    final_r,
    tab_s,
    tab_r,
    sel_s,
    sel_r,
    uprow_s,
    uprow_r,
    low_s,
    low_r,
):
    r = lax.axis_index("req")
    m = lax.axis_index("mlp")
    chips = n_mlp // 2
    y = m // 2
    c = m % 2
    lines = n_req // chips
    z = r // chips
    x = r % chips
    nq = lens.shape[0]
    slot = tokens.shape[0] // nq
    width = tokens.shape[1]
    jw = joined_w.shape[1]
    heads = jw // (3 * HD)
    cols = heads * HD
    own = nq // n_mlp
    chunks = chips * own
    moves = migrants.shape[0]
    n_pages = table.shape[1]
    page = pool_v.shape[1]
    pre = n_pages * page
    total = pre + slot
    rank = adown.shape[1]
    rows_per = adown.shape[0]
    hidden = up_w.shape[1]
    partner = m + 1 - 2 * c
    half = width // 2
    half_cols = pl.ds(pl.multiple_of(c * half, 128), half)

    def peer(jj):
        return lax.rem(m + jj, n_mlp)

    def remote(src, dst, s, d, to_r, to_m):
        return pltpu.make_async_remote_copy(
            src_ref=src, dst_ref=dst, send_sem=s, recv_sem=d, device_id=(to_r, to_m), device_id_type=MESH
        )

    loads = {
        "pool": pltpu.make_async_copy(pool, pool_v, load_sem.at[0]),
        "joined": pltpu.make_async_copy(joined_w, w_one.at[pl.ds(0, width), pl.ds(0, jw)], load_sem.at[1]),
        "dense": pltpu.make_async_copy(dense_w, w_dense, load_sem.at[2]),
        "up": pltpu.make_async_copy(up_w, w_up, load_sem.at[3]),
        "down": pltpu.make_async_copy(down_w, w_one.at[pl.ds(0, hidden), pl.ds(0, width)], load_sem.at[4]),
        "adown": pltpu.make_async_copy(adown, tab.at[z, :, :, pl.ds(0, cols)], load_sem.at[5]),
        "aup": pltpu.make_async_copy(
            aup.at[:, :, half_cols], tab.at[z, :, :, pl.ds(cols, half)], load_sem.at[6]
        ),
    }

    def first_chip(t):
        return rem(y + div(t, own), chips)

    def request(chip, core, s):
        return chip * (2 * own) + core * own + s

    def tok_copy(t, h):
        q = request(first_chip(t), h, rem(t, own))
        return pltpu.make_async_copy(
            tokens.at[pl.ds(pl.multiple_of(q * slot, slot), slot)],
            tok.at[rem(t, 2), pl.ds(h * slot, slot)],
            tok_sem.at[rem(t, 2), h],
        )

    for h in range(2):
        tok_copy(0, h).start()
    loads["adown"].start()
    loads["aup"].start()
    loads["joined"].start()
    res_loads = []
    for chip in range(chips):
        for s in range(own):
            q = request(chip, c, s)
            res_loads.append(
                pltpu.make_async_copy(
                    tokens.at[pl.ds(pl.multiple_of(q * slot, slot), slot)],
                    res.at[chip * own + s],
                    res_sem.at[chip * own + s],
                )
            )

    barrier = pltpu.get_barrier_semaphore()
    for k in range(1, n_req):
        pl.semaphore_signal(barrier, inc=1, device_id=(lax.rem(r + k, n_req), m), device_id_type=MESH)
    for k in range(1, n_mlp):
        pl.semaphore_signal(barrier, inc=1, device_id=(r, peer(k)), device_id_type=MESH)

    key_at = (lax.broadcasted_iota(jnp.int32, (1, total), 1) - pre).astype(F32)
    mine = pl.ds(pl.multiple_of(c * slot, slot), slot)
    theirs = pl.ds(pl.multiple_of((1 - c) * slot, slot), slot)

    def norm_tokens(t):
        for h in range(2):
            tok_copy(t, h).wait()
        b = rem(t, 2)

        def one(i):
            at = pl.ds(pl.multiple_of(i * 64, 64), 64)
            tok[b, at] = layer_norm(tok[b, at].astype(F32), gain_one[...])

        loop(2 * slot // 64, one)

    def project(t):
        b = rem(t, 2)
        tile = jw // 2 if jw % 256 == 0 else jw

        def one(i):
            at = pl.ds(pl.multiple_of(i * tile, tile), tile)
            joined[:, at] = jnp.dot(
                tok[b], w_one[pl.ds(0, width), at], preferred_element_type=F32
            ).astype(BF16)

        loop(jw // tile, one)

    def attend(t, h):
        q = request(first_chip(t), h, rem(t, own))
        length = lens[q]
        g = groups[q]
        rows = pl.ds(pl.multiple_of(h * slot, slot), slot)
        own_row = lax.broadcasted_iota(jnp.int32, (slot, slot), 0)
        own_col = lax.broadcasted_iota(jnp.int32, (slot, slot), 1)
        allowed = (own_col <= own_row) & (own_col < length)
        valid = lax.broadcasted_iota(jnp.int32, (slot, 2 * HD), 0) < length
        pages = [table[g, p] for p in range(n_pages)]
        values, scores, mixed = [], [], []
        for k in range(heads):
            at = k * 3 * HD
            query = joined[rows, at : at + HD]
            kv = joined[rows, at + HD : at + 3 * HD]
            fresh[q, :, k * 2 * HD : (k + 1) * 2 * HD] = jnp.where(valid, kv, jnp.zeros((), BF16))
            keys = jnp.concatenate(
                [pool_v[i, :, k * 2 * HD : k * 2 * HD + HD] for i in pages] + [kv[:, :HD]], axis=0
            )
            values.append(
                jnp.concatenate(
                    [pool_v[i, :, k * 2 * HD + HD : (k + 1) * 2 * HD] for i in pages] + [kv[:, HD:]], axis=0
                )
            )
            scores.append(
                lax.dot_general(query, keys, (((1,), (1,)), ((), ())), preferred_element_type=F32)
            )
        for k in range(heads):
            slope = jnp.float32(0.0)
            for i in range(n_mlp):
                here = 2.0 ** (-8.0 * (i * heads + k + 1.0) / HEADS) * LOG2E
                slope = jnp.where(m == i, jnp.float32(here), slope)
            score = scores[k] * (LOG2E / math.sqrt(HD)) + slope * key_at
            score = jnp.concatenate(
                [score[:, :pre], jnp.where(allowed, score[:, pre:], -jnp.inf)], axis=1
            )
            top = jnp.max(score, axis=-1, keepdims=True)
            weights = jnp.exp2(score - top)
            inverse = 1.0 / jnp.sum(weights, axis=-1, keepdims=True)
            weights = (weights * inverse).astype(BF16)
            mixed.append(jnp.dot(weights, values[k], preferred_element_type=F32))
        for k in range(heads):
            att[t, rows, k * HD : (k + 1) * HD] = mixed[k].astype(BF16)

    def part_copy(t):
        b = rem(t, 2)
        return remote(part.at[b, theirs], part_in.at[b], part_s.at[b], part_r.at[b], r, partner)

    def dense(t):
        b = rem(t, 2)
        tile = min(1024, width)

        def one(i):
            at = pl.ds(pl.multiple_of(i * tile, tile), tile)
            part[b, :, at] = jnp.dot(att[t], w_dense[:, at], preferred_element_type=F32).astype(BF16)

        loop(width // tile, one)

    def pair_copy(t, jy):
        at = first_chip(t) * own + rem(t, own)
        return remote(
            pair_own.at[at], pair_in.at[jy - 1, at], pair_s.at[t, jy - 1], pair_r.at[jy - 1, at], r, peer(2 * jy)
        )

    def pair_arrive(jy, at):
        return remote(
            pair_own.at[at], pair_in.at[jy - 1, at], pair_s.at[0, jy - 1], pair_r.at[jy - 1, at], r, partner
        )

    def pair(t):
        part_copy(t).wait_recv()
        b = rem(t, 2)
        at = first_chip(t) * own + rem(t, own)

        def one(i):
            on = pl.ds(i, 16)
            from_mine = pl.ds(pl.multiple_of(c * slot + i, 16), 16)
            pair_own[at, on] = (part[b, from_mine].astype(F32) + part_in[b, on].astype(F32)).astype(BF16)

        blocks(slot, one)
        for jy in range(1, chips):
            pair_copy(t, jy).start()

    def line_up(step):
        at = jnp.maximum(z - step, 0)
        return (z + 1 < lines) & (z - step >= 0), remote(
            tab.at[at], tab.at[at], tab_s.at[0, step], tab_r.at[at], jnp.minimum(r + chips, n_req - 1), m
        )

    def line_down(step):
        at = jnp.minimum(z + step, lines - 1)
        return (z - 1 >= 0) & (z + step < lines), remote(
            tab.at[at], tab.at[at], tab_s.at[1, step], tab_r.at[at], jnp.maximum(r - chips, 0), m
        )

    def line_arrive(at):
        return remote(tab.at[at], tab.at[at], tab_s.at[0, 0], tab_r.at[at], r, m)

    def line_step(step):
        if step > 0:
            @pl.when(z - step >= 0)
            def _():
                line_arrive(jnp.maximum(z - step, 0)).wait_recv()

            @pl.when(z + step < lines)
            def _():
                line_arrive(jnp.minimum(z + step, lines - 1)).wait_recv()

        if step < lines - 1:
            for go, copy in (line_up(step), line_down(step)):
                @pl.when(go)
                def _(copy=copy):
                    copy.start()

    def line_end():
        for step in range(lines - 1):
            for go, copy in (line_up(step), line_down(step)):
                @pl.when(go)
                def _(copy=copy):
                    copy.wait_send()

    def table_row(request_index):
        return id_rows[ids[request_index]]

    def sel_copy(jx):
        to = z * chips + lax.rem(x + jx, chips)
        return remote(sel_out.at[jx - 1], sel_in.at[jx - 1], sel_s.at[jx - 1], sel_r.at[jx - 1], to, m)

    def select_send():
        for jx in range(1, chips):
            to = z * chips + lax.rem(x + jx, chips)

            def one(q):
                t = table_row(to * nq + q)
                sel_out[jx - 1, q] = tab[div(t, rows_per * chips), rem(t, rows_per)]

            loop(nq, one)
            sel_copy(jx).start()

    def uprow_copy():
        return remote(up_out.at[1 - c], up_rows.at[:, :, half_cols], uprow_s.at[0], uprow_r.at[0], r, partner)

    def select_take():
        for jx in range(1, chips):
            sel_copy(jx).wait_recv()

        def one(q):
            t = table_row(r * nq + q)
            o = div(t, rows_per)
            jx = rem(x - rem(o, chips) + chips, chips)
            here = tab[div(o, chips), rem(t, rows_per)]
            there = sel_in[jnp.maximum(jx - 1, 0), q]
            both = jnp.where(jx == 0, here, there)
            down_rows[q] = both[:, :cols]
            chip, left = div(q, 2 * own), rem(q, 2 * own)
            up_out[div(left, own), chip * own + rem(left, own)] = both[:, cols:]

        loop(nq, one)
        uprow_copy().start()
        up_rows[:, :, half_cols] = up_out[c]

    def low_copy(jj):
        h = lax.rem(c + jj, 2)
        return remote(low_out.at[h], low_in.at[jj - 1], low_s.at[jj - 1], low_r.at[jj - 1], r, peer(jj))

    def low_parts():
        def one(i):
            t, h = div(i, 2), rem(i, 2)
            chip = first_chip(t)
            q = request(chip, h, rem(t, own))
            low_out[h, chip * own + rem(t, own)] = lax.dot_general(
                down_rows[q],
                att[t, pl.ds(pl.multiple_of(h * slot, slot), slot)],
                (((1,), (1,)), ((), ())),
                preferred_element_type=F32,
            ).astype(BF16)

        loop(chunks * 2, one)
        for jj in range(1, n_mlp):
            low_copy(jj).start()

    def mig_copy(j):
        return remote(
            mig_out.at[j - 1], mig_in.at[j - 1], mig_s.at[j - 1], mig_r.at[j - 1], rem(r + j, n_req), m
        )

    def migrate(along):
        def one(i):
            j = i + 1

            @pl.when((rem(j, chips) == 0) == along)
            def _():
                to = rem(r + j, n_req)
                leaving = jnp.int32(0)
                for k in range(moves):
                    leaving = jnp.where(div(landing[r * moves + k], nq) == to, migrants[k], leaving)
                mig_out[j - 1] = fresh[leaving]
                mig_copy(j).start()

        loop(n_req - 1, one)

    def page_copy(s):
        return pltpu.make_async_copy(mig_out.at[s], page_out.at[s], page_sem.at[s])

    def merge():
        for j in range(1, n_req):
            mig_copy(j).wait()

        def one(s):
            def find(k, owner):
                return jnp.where(landing[k] == r * nq + s, div(k, moves), owner)

            owner = lax.fori_loop(0, n_req * moves, find, jnp.int32(-1), unroll=8)
            at = jnp.maximum(rem(r - owner + n_req, n_req) - 1, 0)
            mig_out[s] = jnp.where(owner >= 0, mig_in[at], fresh[s])
            page_copy(s).start()

        loop(nq, one)

    pl.semaphore_wait(barrier, n_req - 1 + n_mlp - 1)
    loads["adown"].wait()
    loads["aup"].wait()
    line_step(0)

    def phase_one(t):
        norm_tokens(t)

        @pl.when(t == 0)
        def _():
            loads["joined"].wait()
            loads["pool"].start()
            loads["dense"].start()
            for h in range(2):
                if chunks > 1:
                    tok_copy(1, h).start()
            for d in res_loads:
                d.start()
            loads["up"].start()

        project(t)

        @pl.when(t + 2 < chunks)
        def _():
            for h in range(2):
                tok_copy(t + 2, h).start()

        @pl.when(t == chunks - 1)
        def _():
            loads["down"].start()

        @pl.when(t > 1)
        def _():
            pair(t - 1)

        @pl.when(t == 0)
        def _():
            loads["pool"].wait()

        loop(2, lambda h: attend(t, h))

        @pl.when(t == 0)
        def _():
            loads["dense"].wait()

        @pl.when(t >= 2)
        def _():
            part_copy(t - 2).wait_send()

        dense(t)
        part_copy(t).start()

        @pl.when(t == 0)
        def _():
            pair(t)

        for step in range(1, min(chunks + 1, lines - 1)):
            @pl.when(t == step - 1)
            def _(step=step):
                line_step(step)

    loop(chunks, phase_one)
    for step in range(min(chunks + 1, lines - 1), lines):
        line_step(step)
    select_send()
    migrate(True)
    select_take()
    low_parts()
    pair(chunks - 1)
    migrate(False)
    uprow_copy().wait_recv()
    for jj in range(1, n_mlp):
        low_copy(jj).wait_recv()
    loads["up"].wait()
    loads["down"].wait()
    for d in res_loads:
        d.wait()

    others = chunks - own

    def second_chip(t):
        return rem(y + 1 + div(t, own), chips)

    def norm_copy(t):
        return remote(normed.at[t, mine], normed.at[t, mine], norm_s.at[t], norm_r.at[t], r, partner)

    def residual(t):
        at = second_chip(t) * own + rem(t, own)
        for jy in range(1, chips):
            pair_arrive(jy, at).wait_recv()
        low = low_out[c, at].astype(F32)
        for jj in range(1, n_mlp):
            low = low + low_in[jj - 1, at].astype(F32)
        low = low.astype(BF16)
        tile = min(512, width)

        def add(i):
            on = pl.ds(pl.multiple_of(i * tile, tile), tile)
            value = res[at, :, on].astype(F32) + pair_own[at, :, on].astype(F32)
            for jy in range(1, chips):
                value = value + pair_in[jy - 1, at, :, on].astype(F32)
            value = value + lax.dot_general(
                low, up_rows[at, :, on], (((0,), (0,)), ((), ())), preferred_element_type=F32
            )
            res[at, :, on] = value.astype(BF16)

        loop(width // tile, add)

        def one(i):
            to = pl.ds(pl.multiple_of(c * slot + i * 64, 64), 64)
            on = pl.ds(pl.multiple_of(i * 64, 64), 64)
            normed[t, to] = layer_norm(res[at, on].astype(F32), gain_two[...])

        loop(slot // 64, one)
        norm_copy(t).start()

    def expand(t):
        norm_copy(t).wait_recv()
        tile = min(1024, hidden)

        def one(i):
            at = pl.ds(pl.multiple_of(i * tile, tile), tile)
            expanded[:, at] = gelu_tanh(
                jnp.dot(normed[t], w_up[:, at], preferred_element_type=F32)
            ).astype(BF16)

        loop(hidden // tile, one)

    def feed_copy(t):
        b = rem(t, 2)
        return remote(feed.at[b, theirs], feed_in.at[t], feed_s.at[t], feed_r.at[t], r, partner)

    def contract(t):
        b = rem(t, 2)
        tile = min(1024, width)

        def one(i):
            at = pl.ds(pl.multiple_of(i * tile, tile), tile)
            feed[b, :, at] = jnp.dot(
                expanded[...], w_one[pl.ds(0, hidden), at], preferred_element_type=F32
            ).astype(BF16)

        loop(width // tile, one)
        feed_copy(t).start()

    def final_copy(t):
        return remote(
            pair_feed.at[t],
            final_in.at[div(t, own), rem(t, own)],
            final_s.at[t],
            final_r.at[div(t, own), rem(t, own)],
            r,
            rem(m + 2 + 2 * div(t, own), n_mlp),
        )

    def final_arrive(jy, s):
        return remote(
            pair_feed.at[0], final_in.at[jy - 1, s], final_s.at[0], final_r.at[jy - 1, s], r, partner
        )

    def gather(t):
        feed_copy(t).wait_recv()
        b = rem(t, 2)

        def one(i):
            on = pl.ds(i, 16)
            from_mine = pl.ds(pl.multiple_of(c * slot + i, 16), 16)
            pair_feed[t, on] = (feed[b, from_mine].astype(F32) + feed_in[t, on].astype(F32)).astype(BF16)

        blocks(slot, one)
        final_copy(t).start()

    def phase_two(u):
        @pl.when(u < chunks)
        def _():
            residual(u)

        @pl.when(u > 0)
        def _():
            t = u - 1
            expand(t)

            @pl.when((t > 0) & (t <= others))
            def _():
                gather(t - 1)

            @pl.when(t >= 2)
            def _():
                feed_copy(t - 2).wait_send()

            contract(t)

    loop(chunks + 1, phase_two)
    for t in range(max(chunks - 2, 0), chunks):
        part_copy(t).wait_send()
    for t in range(chunks):
        for jy in range(1, chips):
            pair_copy(t, jy).wait_send()
        norm_copy(t).wait_send()
    line_end()
    for jx in range(1, chips):
        sel_copy(jx).wait_send()
    uprow_copy().wait_send()
    for jj in range(1, n_mlp):
        low_copy(jj).wait_send()
    merge()

    def out_copy(s):
        return pltpu.make_async_copy(
            out_v.at[s], layer_out.at[pl.ds(pl.multiple_of(s * slot, slot), slot)], out_sem.at[s]
        )

    def finish(s):
        t = others + s
        b = rem(t, 2)
        at = y * own + s
        feed_copy(t).wait_recv()
        for jy in range(1, chips):
            final_arrive(jy, s).wait_recv()
        length = lens[m * own + s]

        def one(i):
            on = pl.ds(i, 16)
            from_mine = pl.ds(pl.multiple_of(c * slot + i, 16), 16)
            value = res[at, on].astype(F32) + (feed[b, from_mine].astype(F32) + feed_in[t, on].astype(F32))
            for jy in range(1, chips):
                value = value + final_in[jy - 1, s, on].astype(F32)
            valid = lax.broadcasted_iota(jnp.int32, (16, width), 0) + i < length
            out_v[s, on] = jnp.where(valid, value, 0.0).astype(BF16)

        blocks(slot, one)
        out_copy(s).start()

    loop(own, finish)
    for t in range(others):
        final_copy(t).wait_send()
    for t in range(max(chunks - 2, 0), chunks):
        feed_copy(t).wait_send()
    for s in range(own):
        out_copy(s).wait()
    for s in range(nq):
        page_copy(s).wait()


def copy_body(first_in, second_in, first_out, second_out, first_v, second_v, sems):
    comes, goes = [], []
    for src, mid, dst in ((first_in, first_v, first_out), (second_in, second_v, second_out)):
        rows = src.shape[0] // 4
        for i in range(4):
            at = pl.ds(i * rows, rows)
            comes.append(pltpu.make_async_copy(src.at[at], mid.at[at], sems.at[0, len(comes)]))
            goes.append(pltpu.make_async_copy(mid.at[at], dst.at[at], sems.at[1, len(goes)]))
    for d in comes:
        d.start()
    for come, go in zip(comes, goes):
        come.wait()
        go.start()
    for d in goes:
        d.wait()


def copy_out(first, second):
    hbm = pl.BlockSpec(memory_space=pl.ANY)
    return pl.pallas_call(
        copy_body,
        out_shape=(
            jax.ShapeDtypeStruct(first.shape, first.dtype),
            jax.ShapeDtypeStruct(second.shape, second.dtype),
        ),
        in_specs=[hbm, hbm],
        out_specs=(hbm, hbm),
        scratch_shapes=[
            pltpu.VMEM(first.shape, first.dtype),
            pltpu.VMEM(second.shape, second.dtype),
            pltpu.SemaphoreType.DMA((2, 8)),
        ],
        compiler_params=pltpu.CompilerParams(vmem_limit_bytes=60 * 1024 * 1024),
    )(first, second)


def shards(n_req, n_mlp, *args):
    (
        tokens,
        first_gain,
        joined_weight,
        dense_weight,
        adapter_down,
        adapter_up,
        adapter_ids,
        adapter_rows,
        second_gain,
        up_weight,
        down_weight,
        page_pool,
        page_table,
        group_index,
        lengths,
        migrants,
        landing,
    ) = args
    chips = n_mlp // 2
    lines = n_req // chips
    nq = lengths.shape[0]
    slot = tokens.shape[0] // nq
    width = tokens.shape[1]
    jw = joined_weight.shape[1]
    heads = jw // (3 * HD)
    cols = heads * HD
    own = nq // n_mlp
    chunks = chips * own
    hidden = up_weight.shape[1]
    rank = adapter_down.shape[1]
    kv = page_pool.shape[2]
    dma = pltpu.SemaphoreType.DMA
    vm = pltpu.VMEM
    others = max(chips - 1, 1)
    scratch = [
        vm((max(width, hidden), max(jw, width)), BF16),
        vm((width, hidden), BF16),
        vm(dense_weight.shape, BF16),
        vm(page_pool.shape, BF16),
        vm((2, 2 * slot, width), BF16),
        vm((2 * slot, jw), BF16),
        vm((chunks, 2 * slot, cols), BF16),
        vm((2, 2 * slot, width), BF16),
        vm((2, slot, width), BF16),
        vm((chunks, slot, width), BF16),
        vm((others, chunks, slot, width), BF16),
        vm((nq, slot, kv), BF16),
        vm((max(nq, n_req - 1), slot, kv), BF16),
        vm((n_req - 1, slot, kv), BF16),
        vm((chunks, slot, width), BF16),
        vm((chunks, 2 * slot, width), BF16),
        vm((2 * slot, hidden), BF16),
        vm((2, 2 * slot, width), BF16),
        vm((chunks, slot, width), BF16),
        vm((max(chunks - own, 1), slot, width), BF16),
        vm((others, own, slot, width), BF16),
        vm((own, slot, width), BF16),
        vm((lines, adapter_down.shape[0], rank, cols + width // 2), BF16),
        vm((others, nq, rank, cols + width // 2), BF16),
        vm((others, nq, rank, cols + width // 2), BF16),
        vm((nq, rank, cols), BF16),
        vm((2, chunks, rank, width // 2), BF16),
        vm((chunks, rank, width), BF16),
        vm((2, chunks, rank, slot), BF16),
        vm((n_mlp - 1, chunks, rank, slot), BF16),
        dma((7,)),
        dma((2, 2)),
        dma((chunks,)),
        dma((own,)),
        dma((nq,)),
        dma((2,)),
        dma((2,)),
        dma((chunks, others)),
        dma((others, chunks)),
        dma((n_req - 1,)),
        dma((n_req - 1,)),
        dma((chunks,)),
        dma((chunks,)),
        dma((chunks,)),
        dma((chunks,)),
        dma((chunks,)),
        dma((others, own)),
        dma((2, lines)),
        dma((lines,)),
        dma((others,)),
        dma((others,)),
        dma((1,)),
        dma((1,)),
        dma((n_mlp - 1,)),
        dma((n_mlp - 1,)),
    ]
    smem = pl.BlockSpec(memory_space=pltpu.SMEM)
    vmem = pl.BlockSpec(memory_space=pltpu.VMEM)
    hbm = pl.BlockSpec(memory_space=pl.ANY)
    rows, pages = pl.pallas_call(
        functools.partial(body, n_req, n_mlp),
        out_shape=(
            jax.ShapeDtypeStruct((own * slot, width), BF16),
            jax.ShapeDtypeStruct((nq, slot, kv), BF16),
        ),
        in_specs=[smem] * 7 + [vmem] * 2 + [hbm] * 8,
        out_specs=(hbm, hbm),
        scratch_shapes=scratch,
        compiler_params=pltpu.CompilerParams(
            collective_id=0, has_side_effects=True, vmem_limit_bytes=63 * 1024 * 1024
        ),
    )(
        adapter_ids,
        adapter_rows,
        page_table,
        group_index,
        lengths,
        migrants,
        landing,
        first_gain.reshape(1, -1),
        second_gain.reshape(1, -1),
        tokens,
        joined_weight,
        dense_weight,
        adapter_down,
        adapter_up,
        up_weight,
        down_weight,
        page_pool,
    )
    return copy_out(rows, pages)


def solution(mesh):
    return jax.shard_map(
        functools.partial(shards, mesh.shape["req"], mesh.shape["mlp"]),
        mesh=mesh,
        in_specs=(
            P("req", None),
            P(),
            P(None, "mlp"),
            P("mlp", None),
            P("req", None, "mlp"),
            P("req", None, None),
            P(),
            P(),
            P(),
            P(None, "mlp"),
            P("mlp", None),
            P("req", None, "mlp"),
            P("req", None),
            P("req"),
            P("req"),
            P("req"),
            P(),
        ),
        out_specs=(P(("req", "mlp"), None), P("req", None, "mlp")),
        check_vma=False,
    )
```

```python
import functools
import math

import jax
import jax.numpy as jnp
from jax import lax
from jax.experimental import pallas as pl
from jax.experimental.pallas import tpu as pltpu
from jax.sharding import PartitionSpec as P

HEADS = 16
HD = 128
EPS = 1e-05
LOG2E = 1.4426950408889634
MESH = pl.DeviceIdType.MESH
F32 = jnp.float32
BF16 = jnp.bfloat16


def layer_norm(values, gain):
    mean = jnp.mean(values, axis=-1, keepdims=True)
    centred = values - mean
    variance = jnp.mean(centred * centred, axis=-1, keepdims=True)
    return (centred * lax.rsqrt(variance + EPS) * gain).astype(BF16)


def div(a, b):
    return a // b if isinstance(a, int) else lax.div(a, jnp.int32(b))


def rem(a, b):
    return a % b if isinstance(a, int) else lax.rem(a, jnp.int32(b))


def loop(count, step, unroll=1):
    def one(i, carry):
        step(i)
        return carry

    lax.fori_loop(0, count, one, 0, unroll=unroll)


def blocks(rows, step, unroll=2):
    loop(rows // 16, lambda i: step(i * 16 if isinstance(i, int) else pl.multiple_of(i * 16, 16)), unroll)


def gelu_tanh(value):
    return 0.5 * value * (1.0 + jnp.tanh(0.7978845608 * (value + 0.044715 * value * value * value)))


def body(
    n_req,
    n_mlp,
    ids,
    id_rows,
    table,
    groups,
    lens,
    migrants,
    landing,
    gain_one,
    gain_two,
    tokens,
    joined_w,
    dense_w,
    adown,
    aup,
    up_w,
    down_w,
    pool,
    layer_out,
    page_out,
    w_one,
    w_up,
    w_dense,
    pool_v,
    tok,
    joined,
    att,
    part,
    pair_own,
    pair_in,
    fresh,
    mig_out,
    mig_in,
    res,
    normed,
    expanded,
    feed,
    feed_in,
    pair_feed,
    final_in,
    out_v,
    tab_d,
    sel_out_d,
    sel_in_d,
    tab_u,
    sel_out_u,
    sel_in_u,
    down_rows,
    up_out,
    up_rows,
    low_out,
    low_in,
    load_sem,
    tok_sem,
    res_sem,
    out_sem,
    page_sem,
    part_s,
    part_r,
    pair_s,
    pair_r,
    mig_s,
    mig_r,
    norm_s,
    norm_r,
    feed_s,
    feed_r,
    final_s,
    final_r,
    tab_s,
    tab_r,
    sel_s,
    sel_r,
    uprow_s,
    uprow_r,
    low_s,
    low_r,
):
    r = lax.axis_index("req")
    m = lax.axis_index("mlp")
    chips = n_mlp // 2
    y = m // 2
    c = m % 2
    lines = n_req // chips
    z = r // chips
    x = r % chips
    nq = lens.shape[0]
    slot = tokens.shape[0] // nq
    width = tokens.shape[1]
    jw = joined_w.shape[1]
    heads = jw // (3 * HD)
    cols = heads * HD
    own = nq // n_mlp
    chunks = chips * own
    moves = migrants.shape[0]
    n_pages = table.shape[1]
    page = pool_v.shape[1]
    pre = n_pages * page
    total = pre + slot
    rank = adown.shape[1]
    rows_per = adown.shape[0]
    hidden = up_w.shape[1]
    partner = m + 1 - 2 * c
    half = width // 2
    half_cols = pl.ds(pl.multiple_of(c * half, 128), half)

    def peer(jj):
        return lax.rem(m + jj, n_mlp)

    def remote(src, dst, s, d, to_r, to_m):
        return pltpu.make_async_remote_copy(
            src_ref=src, dst_ref=dst, send_sem=s, recv_sem=d, device_id=(to_r, to_m), device_id_type=MESH
        )

    loads = {
        "pool": pltpu.make_async_copy(pool, pool_v, load_sem.at[0]),
        "joined": pltpu.make_async_copy(joined_w, w_one.at[pl.ds(0, width), pl.ds(0, jw)], load_sem.at[1]),
        "dense": pltpu.make_async_copy(dense_w, w_dense, load_sem.at[2]),
        "up": pltpu.make_async_copy(up_w, w_up, load_sem.at[3]),
        "down": pltpu.make_async_copy(down_w, w_one.at[pl.ds(0, hidden), pl.ds(0, width)], load_sem.at[4]),
        "adown": pltpu.make_async_copy(adown, tab_d.at[z], load_sem.at[5]),
        "aup": pltpu.make_async_copy(aup.at[:, :, half_cols], tab_u.at[z], load_sem.at[6]),
    }
    tabs, sel_outs, sel_ins = (tab_d, tab_u), (sel_out_d, sel_out_u), (sel_in_d, sel_in_u)

    def first_chip(t):
        return rem(y + div(t, own), chips)

    def request(chip, core, s):
        return chip * (2 * own) + core * own + s

    def tok_copy(t, h):
        q = request(first_chip(t), h, rem(t, own))
        return pltpu.make_async_copy(
            tokens.at[pl.ds(pl.multiple_of(q * slot, slot), slot)],
            tok.at[rem(t, 2), pl.ds(h * slot, slot)],
            tok_sem.at[rem(t, 2), h],
        )

    for h in range(2):
        tok_copy(0, h).start()
    loads["adown"].start()
    loads["aup"].start()
    loads["joined"].start()
    res_loads = []
    for chip in range(chips):
        for s in range(own):
            q = request(chip, c, s)
            res_loads.append(
                pltpu.make_async_copy(
                    tokens.at[pl.ds(pl.multiple_of(q * slot, slot), slot)],
                    res.at[chip * own + s],
                    res_sem.at[chip * own + s],
                )
            )

    barrier = pltpu.get_barrier_semaphore()
    for k in range(1, n_req):
        pl.semaphore_signal(barrier, inc=1, device_id=(lax.rem(r + k, n_req), m), device_id_type=MESH)
    for k in range(1, n_mlp):
        pl.semaphore_signal(barrier, inc=1, device_id=(r, peer(k)), device_id_type=MESH)

    key_at = (lax.broadcasted_iota(jnp.int32, (1, total), 1) - pre).astype(F32)
    mine = pl.ds(pl.multiple_of(c * slot, slot), slot)
    theirs = pl.ds(pl.multiple_of((1 - c) * slot, slot), slot)

    def norm_tokens(t):
        for h in range(2):
            tok_copy(t, h).wait()
        b = rem(t, 2)

        def one(i):
            at = pl.ds(pl.multiple_of(i * 64, 64), 64)
            tok[b, at] = layer_norm(tok[b, at].astype(F32), gain_one[...])

        loop(2 * slot // 64, one)

    def project(t):
        b = rem(t, 2)
        tile = jw // 2 if jw % 256 == 0 else jw

        def one(i):
            at = pl.ds(pl.multiple_of(i * tile, tile), tile)
            joined[b, :, at] = jnp.dot(
                tok[b], w_one[pl.ds(0, width), at], preferred_element_type=F32
            ).astype(BF16)

        loop(jw // tile, one)

    def keep(t, h):
        q = request(first_chip(t), h, rem(t, own))
        b = rem(t, 2)
        rows = pl.ds(pl.multiple_of(h * slot, slot), slot)
        valid = lax.broadcasted_iota(jnp.int32, (slot, 2 * HD), 0) < lens[q]
        for k in range(heads):
            at = k * 3 * HD + HD
            fresh[q, :, k * 2 * HD : (k + 1) * 2 * HD] = jnp.where(
                valid, joined[b, rows, at : at + 2 * HD], jnp.zeros((), BF16)
            )

    def attend(t, h):
        q = request(first_chip(t), h, rem(t, own))
        b = rem(t, 2)
        length = lens[q]
        g = groups[q]
        rows = pl.ds(pl.multiple_of(h * slot, slot), slot)
        own_row = lax.broadcasted_iota(jnp.int32, (slot, slot), 0)
        own_col = lax.broadcasted_iota(jnp.int32, (slot, slot), 1)
        allowed = (own_col <= own_row) & (own_col < length)
        pages = [table[g, p] for p in range(n_pages)]
        values, scores, mixed = [], [], []
        for k in range(heads):
            at = k * 3 * HD
            query = joined[b, rows, at : at + HD]
            kv = joined[b, rows, at + HD : at + 3 * HD]
            keys = jnp.concatenate(
                [pool_v[i, :, k * 2 * HD : k * 2 * HD + HD] for i in pages] + [kv[:, :HD]], axis=0
            )
            values.append(
                jnp.concatenate(
                    [pool_v[i, :, k * 2 * HD + HD : (k + 1) * 2 * HD] for i in pages] + [kv[:, HD:]], axis=0
                )
            )
            scores.append(
                lax.dot_general(query, keys, (((1,), (1,)), ((), ())), preferred_element_type=F32)
            )
        for k in range(heads):
            slope = jnp.float32(0.0)
            for i in range(n_mlp):
                here = 2.0 ** (-8.0 * (i * heads + k + 1.0) / HEADS) * LOG2E
                slope = jnp.where(m == i, jnp.float32(here), slope)
            score = scores[k] * (LOG2E / math.sqrt(HD)) + slope * key_at
            score = jnp.concatenate(
                [score[:, :pre], jnp.where(allowed, score[:, pre:], -jnp.inf)], axis=1
            )
            top = jnp.max(score, axis=-1, keepdims=True)
            weights = jnp.exp2(score - top)
            inverse = 1.0 / jnp.sum(weights, axis=-1, keepdims=True)
            weights = (weights * inverse).astype(BF16)
            mixed.append(jnp.dot(weights, values[k], preferred_element_type=F32))
        for k in range(heads):
            att[t, rows, k * HD : (k + 1) * HD] = mixed[k].astype(BF16)

    def part_copy(t):
        b = rem(t, 2)
        return remote(part.at[b, theirs], feed_in.at[t], part_s.at[t], part_r.at[t], r, partner)

    def dense(t):
        b = rem(t, 2)
        tile = min(1024, width)

        def one(i):
            at = pl.ds(pl.multiple_of(i * tile, tile), tile)
            part[b, :, at] = jnp.dot(att[t], w_dense[:, at], preferred_element_type=F32).astype(BF16)

        loop(width // tile, one)

    def pair_copy(t, jy):
        at = first_chip(t) * own + rem(t, own)
        return remote(
            pair_own.at[at], pair_in.at[jy - 1, at], pair_s.at[t, jy - 1], pair_r.at[jy - 1, at], r, peer(2 * jy)
        )

    def pair_arrive(jy, at):
        return remote(
            pair_own.at[at], pair_in.at[jy - 1, at], pair_s.at[0, jy - 1], pair_r.at[jy - 1, at], r, partner
        )

    def pair(t):
        part_copy(t).wait_recv()
        b = rem(t, 2)
        at = first_chip(t) * own + rem(t, own)

        def one(i):
            on = pl.ds(i, 16)
            from_mine = pl.ds(pl.multiple_of(c * slot + i, 16), 16)
            pair_own[at, on] = (part[b, from_mine].astype(F32) + feed_in[t, on].astype(F32)).astype(BF16)

        blocks(slot, one)
        for jy in range(1, chips):
            pair_copy(t, jy).start()

    def line_up(kind, step):
        at = jnp.maximum(z - step, 0)
        return (z + 1 < lines) & (z - step >= 0), remote(
            tabs[kind].at[at],
            tabs[kind].at[at],
            tab_s.at[kind, 0, step],
            tab_r.at[kind, at],
            jnp.minimum(r + chips, n_req - 1),
            m,
        )

    def line_down(kind, step):
        at = jnp.minimum(z + step, lines - 1)
        return (z - 1 >= 0) & (z + step < lines), remote(
            tabs[kind].at[at],
            tabs[kind].at[at],
            tab_s.at[kind, 1, step],
            tab_r.at[kind, at],
            jnp.maximum(r - chips, 0),
            m,
        )

    def line_arrive(kind, at):
        return remote(tabs[kind].at[at], tabs[kind].at[at], tab_s.at[kind, 0, 0], tab_r.at[kind, at], r, m)

    def line_step(kind, step):
        if step > 0:
            @pl.when(z - step >= 0)
            def _():
                line_arrive(kind, jnp.maximum(z - step, 0)).wait_recv()

            @pl.when(z + step < lines)
            def _():
                line_arrive(kind, jnp.minimum(z + step, lines - 1)).wait_recv()

        if step < lines - 1:
            for go, copy in (line_up(kind, step), line_down(kind, step)):
                @pl.when(go)
                def _(copy=copy):
                    copy.start()

    def line_point(kind, place):
        for step in range(1, lines):
            if min(step, 3) == place:
                line_step(kind, step)

    def line_end():
        for kind in range(2):
            for step in range(lines - 1):
                for go, copy in (line_up(kind, step), line_down(kind, step)):
                    @pl.when(go)
                    def _(copy=copy):
                        copy.wait_send()

    def table_row(request_index):
        return id_rows[ids[request_index]]

    def sel_copy(kind, jx):
        to = z * chips + lax.rem(x + jx, chips)
        return remote(
            sel_outs[kind].at[jx - 1],
            sel_ins[kind].at[jx - 1],
            sel_s.at[kind, jx - 1],
            sel_r.at[kind, jx - 1],
            to,
            m,
        )

    def select_send(kind):
        for jx in range(1, chips):
            to = z * chips + lax.rem(x + jx, chips)

            def one(q):
                t = table_row(to * nq + q)
                sel_outs[kind][jx - 1, q] = tabs[kind][div(t, rows_per * chips), rem(t, rows_per)]

            loop(nq, one)
            sel_copy(kind, jx).start()

    def select_take(kind):
        for jx in range(1, chips):
            sel_copy(kind, jx).wait_recv()

        def one(q):
            t = table_row(r * nq + q)
            o = div(t, rows_per)
            jx = rem(x - rem(o, chips) + chips, chips)
            here = tabs[kind][div(o, chips), rem(t, rows_per)]
            there = sel_ins[kind][jnp.maximum(jx - 1, 0), q]
            both = jnp.where(jx == 0, here, there)
            if kind == 0:
                down_rows[q] = both
            else:
                chip, left = div(q, 2 * own), rem(q, 2 * own)
                up_out[div(left, own), chip * own + rem(left, own)] = both

        loop(nq, one)
        if kind == 1:
            uprow_copy().start()
            up_rows[:, :, half_cols] = up_out[c]

    def uprow_copy():
        return remote(up_out.at[1 - c], up_rows.at[:, :, half_cols], uprow_s.at[0], uprow_r.at[0], r, partner)

    def low_copy(jj):
        h = lax.rem(c + jj, 2)
        return remote(low_out.at[h], low_in.at[jj - 1], low_s.at[jj - 1], low_r.at[jj - 1], r, peer(jj))

    def low_parts():
        def one(i):
            t, h = div(i, 2), rem(i, 2)
            chip = first_chip(t)
            q = request(chip, h, rem(t, own))
            low_out[h, chip * own + rem(t, own)] = lax.dot_general(
                down_rows[q],
                att[t, pl.ds(pl.multiple_of(h * slot, slot), slot)],
                (((1,), (1,)), ((), ())),
                preferred_element_type=F32,
            ).astype(BF16)

        loop(chunks * 2, one)
        for jj in range(1, n_mlp):
            low_copy(jj).start()

    def mig_copy(j):
        return remote(
            mig_out.at[j - 1], mig_in.at[j - 1], mig_s.at[j - 1], mig_r.at[j - 1], rem(r + j, n_req), m
        )

    def migrate(along):
        def one(i):
            j = i + 1

            @pl.when((rem(j, chips) == 0) == along)
            def _():
                to = rem(r + j, n_req)
                leaving = jnp.int32(0)
                for k in range(moves):
                    leaving = jnp.where(div(landing[r * moves + k], nq) == to, migrants[k], leaving)
                mig_out[j - 1] = fresh[leaving]
                mig_copy(j).start()

        loop(n_req - 1, one)

    def page_copy(s):
        return pltpu.make_async_copy(mig_out.at[s], page_out.at[s], page_sem.at[s])

    def merge():
        for j in range(1, n_req):
            mig_copy(j).wait()

        def one(s):
            def find(k, owner):
                return jnp.where(landing[k] == r * nq + s, div(k, moves), owner)

            owner = lax.fori_loop(0, n_req * moves, find, jnp.int32(-1), unroll=8)
            at = jnp.maximum(rem(r - owner + n_req, n_req) - 1, 0)
            mig_out[s] = jnp.where(owner >= 0, mig_in[at], fresh[s])
            page_copy(s).start()

        loop(nq, one)

    norm_tokens(0)
    pl.semaphore_wait(barrier, n_req - 1 + n_mlp - 1)
    loads["adown"].wait()
    loads["aup"].wait()
    line_step(1, 0)

    def phase_one(u):
        @pl.when(u < chunks)
        def _():
            t = u

            @pl.when(t > 0)
            def _():
                norm_tokens(t)

            @pl.when(t == 0)
            def _():
                loads["joined"].wait()
                loads["pool"].start()
                loads["dense"].start()
                for h in range(2):
                    if chunks > 1:
                        tok_copy(1, h).start()
                for d in res_loads:
                    d.start()
                loads["up"].start()

            project(t)

            @pl.when(t + 2 < chunks)
            def _():
                for h in range(2):
                    tok_copy(t + 2, h).start()

            @pl.when(t == 0)
            def _():
                line_step(0, 0)
                loads["pool"].wait()

            @pl.when(t == 1)
            def _():
                loop(2, lambda h: keep(0, h))

            @pl.when(t > 0)
            def _():
                loop(2, lambda h: keep(t, h))

            @pl.when(t == chunks - 1)
            def _():
                loads["down"].start()
                line_point(0, 3)
                select_send(0)
                migrate(True)

        @pl.when(u != 1)
        def _():
            t = u - (u > 1).astype(jnp.int32)
            loop(2, lambda h: attend(t, h))

            @pl.when(t == 0)
            def _():
                loads["dense"].wait()

            @pl.when(t >= 2)
            def _():
                part_copy(t - 2).wait_send()

            dense(t)
            part_copy(t).start()

            @pl.when(t == 0)
            def _():
                line_point(1, 1)

            @pl.when(t < 2)
            def _():
                pair(t)

        @pl.when(u == 1)
        def _():
            line_point(1, 2)
            line_point(0, 1)

        @pl.when(u == 2)
        def _():
            line_point(1, 3)
            select_send(1)
            line_point(0, 2)

    loop(chunks + 1, phase_one)
    select_take(0)
    low_parts()
    for t in range(2, chunks):
        pair(t)
    select_take(1)
    migrate(False)
    uprow_copy().wait_recv()
    for jj in range(1, n_mlp):
        low_copy(jj).wait_recv()
    loads["up"].wait()
    loads["down"].wait()
    for d in res_loads:
        d.wait()

    others = chunks - own

    def second_chip(t):
        return rem(y + 1 + div(t, own), chips)

    def norm_copy(t):
        return remote(normed.at[t, mine], normed.at[t, mine], norm_s.at[t], norm_r.at[t], r, partner)

    def residual(t):
        at = second_chip(t) * own + rem(t, own)
        for jy in range(1, chips):
            pair_arrive(jy, at).wait_recv()
        low = low_out[c, at].astype(F32)
        for jj in range(1, n_mlp):
            low = low + low_in[jj - 1, at].astype(F32)
        low = low.astype(BF16)
        tile = min(512, width)

        def add(i):
            on = pl.ds(pl.multiple_of(i * tile, tile), tile)
            value = res[at, :, on].astype(F32) + pair_own[at, :, on].astype(F32)
            for jy in range(1, chips):
                value = value + pair_in[jy - 1, at, :, on].astype(F32)
            value = value + lax.dot_general(
                low, up_rows[at, :, on], (((0,), (0,)), ((), ())), preferred_element_type=F32
            )
            res[at, :, on] = value.astype(BF16)

        loop(width // tile, add)

        def one(i):
            to = pl.ds(pl.multiple_of(c * slot + i * 64, 64), 64)
            on = pl.ds(pl.multiple_of(i * 64, 64), 64)
            normed[t, to] = layer_norm(res[at, on].astype(F32), gain_two[...])

        loop(slot // 64, one)
        norm_copy(t).start()

    def expand(t):
        norm_copy(t).wait_recv()
        tile = min(1024, hidden)

        def one(i):
            at = pl.ds(pl.multiple_of(i * tile, tile), tile)
            expanded[:, at] = gelu_tanh(
                jnp.dot(normed[t], w_up[:, at], preferred_element_type=F32)
            ).astype(BF16)

        loop(hidden // tile, one)

    def feed_copy(t):
        b = rem(t, 2)
        return remote(feed.at[b, theirs], feed_in.at[t], feed_s.at[t], feed_r.at[t], r, partner)

    def contract(t):
        b = rem(t, 2)
        tile = min(1024, width)

        def one(i):
            at = pl.ds(pl.multiple_of(i * tile, tile), tile)
            feed[b, :, at] = jnp.dot(
                expanded[...], w_one[pl.ds(0, hidden), at], preferred_element_type=F32
            ).astype(BF16)

        loop(width // tile, one)
        feed_copy(t).start()

    def final_copy(t, p):
        on = pl.ds(p * (slot // 2), slot // 2)
        return remote(
            pair_feed.at[t, on],
            final_in.at[div(t, own), rem(t, own), on],
            final_s.at[t, p],
            final_r.at[div(t, own), rem(t, own), p],
            r,
            rem(m + 2 + 2 * div(t, own), n_mlp),
        )

    def final_arrive(jy, s, p):
        on = pl.ds(pl.multiple_of(p * (slot // 2), 16), slot // 2)
        return remote(
            pair_feed.at[0, on],
            final_in.at[jy - 1, s, on],
            final_s.at[0, p],
            final_r.at[jy - 1, s, p],
            r,
            partner,
        )

    def gather(t):
        feed_copy(t).wait_recv()
        b = rem(t, 2)

        def one(i):
            on = pl.ds(i, 16)
            from_mine = pl.ds(pl.multiple_of(c * slot + i, 16), 16)
            pair_feed[t, on] = (feed[b, from_mine].astype(F32) + feed_in[t, on].astype(F32)).astype(BF16)

        blocks(slot, one)
        for p in range(2):
            final_copy(t, p).start()

    def phase_two(u):
        @pl.when(u < chunks)
        def _():
            residual(u)

        @pl.when(u > 0)
        def _():
            t = u - 1
            expand(t)

            @pl.when(t >= 2)
            def _():
                feed_copy(t - 2).wait_send()

            contract(t)

            @pl.when(t < others)
            def _():
                gather(t)

    loop(chunks + 1, phase_two)
    for t in range(max(chunks - 2, 0), chunks):
        part_copy(t).wait_send()
    for t in range(chunks):
        for jy in range(1, chips):
            pair_copy(t, jy).wait_send()
        norm_copy(t).wait_send()
    line_end()
    for kind in range(2):
        for jx in range(1, chips):
            sel_copy(kind, jx).wait_send()
    uprow_copy().wait_send()
    for jj in range(1, n_mlp):
        low_copy(jj).wait_send()
    merge()

    def out_copy(s, p):
        on = pl.ds(pl.multiple_of(p * (slot // 2), 16), slot // 2)
        to = pl.ds(pl.multiple_of(s * slot + p * (slot // 2), 16), slot // 2)
        return pltpu.make_async_copy(out_v.at[s, on], layer_out.at[to], out_sem.at[s, p])

    def finish(k):
        s, p = div(k, 2), rem(k, 2)
        t = others + s
        b = rem(t, 2)
        at = y * own + s

        @pl.when(p == 0)
        def _():
            feed_copy(t).wait_recv()

        for jy in range(1, chips):
            final_arrive(jy, s, p).wait_recv()
        length = lens[m * own + s]

        def one(i):
            row = p * (slot // 2) + i
            on = pl.ds(pl.multiple_of(row, 16), 16)
            from_mine = pl.ds(pl.multiple_of(c * slot + row, 16), 16)
            value = res[at, on].astype(F32) + (feed[b, from_mine].astype(F32) + feed_in[t, on].astype(F32))
            for jy in range(1, chips):
                value = value + final_in[jy - 1, s, on].astype(F32)
            valid = lax.broadcasted_iota(jnp.int32, (16, width), 0) + row < length
            out_v[s, on] = jnp.where(valid, value, 0.0).astype(BF16)

        blocks(slot // 2, one)
        out_copy(s, p).start()

    loop(own * 2, finish)
    for t in range(others):
        for p in range(2):
            final_copy(t, p).wait_send()
    for t in range(max(chunks - 2, 0), chunks):
        feed_copy(t).wait_send()
    for s in range(own):
        for p in range(2):
            out_copy(s, p).wait()
    for s in range(nq):
        page_copy(s).wait()


def copy_body(first_in, second_in, first_out, second_out, first_v, second_v, sems):
    comes, goes = [], []
    for src, mid, dst in ((first_in, first_v, first_out), (second_in, second_v, second_out)):
        rows = src.shape[0] // 4
        for i in range(4):
            at = pl.ds(i * rows, rows)
            comes.append(pltpu.make_async_copy(src.at[at], mid.at[at], sems.at[0, len(comes)]))
            goes.append(pltpu.make_async_copy(mid.at[at], dst.at[at], sems.at[1, len(goes)]))
    for d in comes:
        d.start()
    for come, go in zip(comes, goes):
        come.wait()
        go.start()
    for d in goes:
        d.wait()


def copy_out(first, second):
    hbm = pl.BlockSpec(memory_space=pl.ANY)
    return pl.pallas_call(
        copy_body,
        out_shape=(
            jax.ShapeDtypeStruct(first.shape, first.dtype),
            jax.ShapeDtypeStruct(second.shape, second.dtype),
        ),
        in_specs=[hbm, hbm],
        out_specs=(hbm, hbm),
        scratch_shapes=[
            pltpu.VMEM(first.shape, first.dtype),
            pltpu.VMEM(second.shape, second.dtype),
            pltpu.SemaphoreType.DMA((2, 8)),
        ],
        compiler_params=pltpu.CompilerParams(vmem_limit_bytes=60 * 1024 * 1024),
    )(first, second)


def shards(n_req, n_mlp, *args):
    (
        tokens,
        first_gain,
        joined_weight,
        dense_weight,
        adapter_down,
        adapter_up,
        adapter_ids,
        adapter_rows,
        second_gain,
        up_weight,
        down_weight,
        page_pool,
        page_table,
        group_index,
        lengths,
        migrants,
        landing,
    ) = args
    chips = n_mlp // 2
    lines = n_req // chips
    nq = lengths.shape[0]
    slot = tokens.shape[0] // nq
    width = tokens.shape[1]
    jw = joined_weight.shape[1]
    heads = jw // (3 * HD)
    cols = heads * HD
    own = nq // n_mlp
    chunks = chips * own
    hidden = up_weight.shape[1]
    rank = adapter_down.shape[1]
    kv = page_pool.shape[2]
    dma = pltpu.SemaphoreType.DMA
    vm = pltpu.VMEM
    others = max(chips - 1, 1)
    scratch = [
        vm((max(width, hidden), max(jw, width)), BF16),
        vm((width, hidden), BF16),
        vm(dense_weight.shape, BF16),
        vm(page_pool.shape, BF16),
        vm((2, 2 * slot, width), BF16),
        vm((2, 2 * slot, jw), BF16),
        vm((chunks, 2 * slot, cols), BF16),
        vm((2, 2 * slot, width), BF16),
        vm((chunks, slot, width), BF16),
        vm((others, chunks, slot, width), BF16),
        vm((nq, slot, kv), BF16),
        vm((max(nq, n_req - 1), slot, kv), BF16),
        vm((n_req - 1, slot, kv), BF16),
        vm((chunks, slot, width), BF16),
        vm((chunks, 2 * slot, width), BF16),
        vm((2 * slot, hidden), BF16),
        vm((2, 2 * slot, width), BF16),
        vm((chunks, slot, width), BF16),
        vm((max(chunks - own, 1), slot, width), BF16),
        vm((others, own, slot, width), BF16),
        vm((own, slot, width), BF16),
        vm((lines, adapter_down.shape[0], rank, cols), BF16),
        vm((others, nq, rank, cols), BF16),
        vm((others, nq, rank, cols), BF16),
        vm((lines, adapter_down.shape[0], rank, width // 2), BF16),
        vm((others, nq, rank, width // 2), BF16),
        vm((others, nq, rank, width // 2), BF16),
        vm((nq, rank, cols), BF16),
        vm((2, chunks, rank, width // 2), BF16),
        vm((chunks, rank, width), BF16),
        vm((2, chunks, rank, slot), BF16),
        vm((n_mlp - 1, chunks, rank, slot), BF16),
        dma((7,)),
        dma((2, 2)),
        dma((chunks,)),
        dma((own, 2)),
        dma((nq,)),
        dma((chunks,)),
        dma((chunks,)),
        dma((chunks, others)),
        dma((others, chunks)),
        dma((n_req - 1,)),
        dma((n_req - 1,)),
        dma((chunks,)),
        dma((chunks,)),
        dma((chunks,)),
        dma((chunks,)),
        dma((chunks, 2)),
        dma((others, own, 2)),
        dma((2, 2, lines)),
        dma((2, lines)),
        dma((2, others)),
        dma((2, others)),
        dma((1,)),
        dma((1,)),
        dma((n_mlp - 1,)),
        dma((n_mlp - 1,)),
    ]
    smem = pl.BlockSpec(memory_space=pltpu.SMEM)
    vmem = pl.BlockSpec(memory_space=pltpu.VMEM)
    hbm = pl.BlockSpec(memory_space=pl.ANY)
    rows, pages = pl.pallas_call(
        functools.partial(body, n_req, n_mlp),
        out_shape=(
            jax.ShapeDtypeStruct((own * slot, width), BF16),
            jax.ShapeDtypeStruct((nq, slot, kv), BF16),
        ),
        in_specs=[smem] * 7 + [vmem] * 2 + [hbm] * 8,
        out_specs=(hbm, hbm),
        scratch_shapes=scratch,
        compiler_params=pltpu.CompilerParams(
            collective_id=0, has_side_effects=True, vmem_limit_bytes=63 * 1024 * 1024
        ),
    )(
        adapter_ids,
        adapter_rows,
        page_table,
        group_index,
        lengths,
        migrants,
        landing,
        first_gain.reshape(1, -1),
        second_gain.reshape(1, -1),
        tokens,
        joined_weight,
        dense_weight,
        adapter_down,
        adapter_up,
        up_weight,
        down_weight,
        page_pool,
    )
    return copy_out(rows, pages)


def solution(mesh):
    return jax.shard_map(
        functools.partial(shards, mesh.shape["req"], mesh.shape["mlp"]),
        mesh=mesh,
        in_specs=(
            P("req", None),
            P(),
            P(None, "mlp"),
            P("mlp", None),
            P("req", None, "mlp"),
            P("req", None, None),
            P(),
            P(),
            P(),
            P(None, "mlp"),
            P("mlp", None),
            P("req", None, "mlp"),
            P("req", None),
            P("req"),
            P("req"),
            P("req"),
            P(),
        ),
        out_specs=(P(("req", "mlp"), None), P("req", None, "mlp")),
        check_vma=False,
    )
```

```python
import functools
import math

import jax
import jax.numpy as jnp
from jax import lax
from jax.experimental import pallas as pl
from jax.experimental.pallas import tpu as pltpu
from jax.sharding import PartitionSpec as P

HEADS = 16
HD = 128
EPS = 1e-05
LOG2E = 1.4426950408889634
MESH = pl.DeviceIdType.MESH
F32 = jnp.float32
BF16 = jnp.bfloat16


def layer_norm(values, gain):
    mean = jnp.mean(values, axis=-1, keepdims=True)
    centred = values - mean
    variance = jnp.mean(centred * centred, axis=-1, keepdims=True)
    return (centred * lax.rsqrt(variance + EPS) * gain).astype(BF16)


def div(a, b):
    return a // b if isinstance(a, int) else lax.div(a, jnp.int32(b))


def rem(a, b):
    return a % b if isinstance(a, int) else lax.rem(a, jnp.int32(b))


def loop(count, step, unroll=1):
    def one(i, carry):
        step(i)
        return carry

    lax.fori_loop(0, count, one, 0, unroll=unroll)


def blocks(rows, step, unroll=2):
    loop(rows // 16, lambda i: step(i * 16 if isinstance(i, int) else pl.multiple_of(i * 16, 16)), unroll)


def gelu_tanh(value):
    return 0.5 * value * (1.0 + jnp.tanh(0.7978845608 * (value + 0.044715 * value * value * value)))


def body(
    n_req,
    n_mlp,
    ids,
    id_rows,
    table,
    groups,
    lens,
    migrants,
    landing,
    gain_one,
    gain_two,
    tokens,
    joined_w,
    dense_w,
    adown,
    aup,
    up_w,
    down_w,
    pool,
    layer_out,
    page_out,
    w_one,
    w_up,
    w_dense,
    pool_v,
    tok,
    joined,
    att,
    part,
    pair_own,
    pair_in,
    fresh,
    mig_out,
    mig_in,
    res,
    normed,
    expanded,
    feed,
    feed_in,
    pair_feed,
    final_in,
    out_v,
    tab_d,
    sel_out_d,
    sel_in_d,
    tab_u,
    sel_out_u,
    sel_in_u,
    down_rows,
    up_out,
    up_rows,
    low_out,
    low_in,
    load_sem,
    tok_sem,
    res_sem,
    out_sem,
    page_sem,
    part_s,
    part_r,
    pair_s,
    pair_r,
    mig_s,
    mig_r,
    norm_s,
    norm_r,
    feed_s,
    feed_r,
    final_s,
    final_r,
    tab_s,
    tab_r,
    sel_s,
    sel_r,
    uprow_s,
    uprow_r,
    low_s,
    low_r,
):
    r = lax.axis_index("req")
    m = lax.axis_index("mlp")
    chips = n_mlp // 2
    y = m // 2
    c = m % 2
    lines = n_req // chips
    z = r // chips
    x = r % chips
    nq = lens.shape[0]
    slot = tokens.shape[0] // nq
    width = tokens.shape[1]
    jw = joined_w.shape[1]
    heads = jw // (3 * HD)
    cols = heads * HD
    own = nq // n_mlp
    chunks = chips * own
    moves = migrants.shape[0]
    n_pages = table.shape[1]
    page = pool_v.shape[1]
    pre = n_pages * page
    total = pre + slot
    rank = adown.shape[1]
    rows_per = adown.shape[0]
    hidden = up_w.shape[1]
    partner = m + 1 - 2 * c
    half = width // 2
    half_cols = pl.ds(pl.multiple_of(c * half, 128), half)

    def peer(jj):
        return lax.rem(m + jj, n_mlp)

    def remote(src, dst, s, d, to_r, to_m):
        return pltpu.make_async_remote_copy(
            src_ref=src, dst_ref=dst, send_sem=s, recv_sem=d, device_id=(to_r, to_m), device_id_type=MESH
        )

    loads = {
        "pool": pltpu.make_async_copy(pool, pool_v, load_sem.at[0]),
        "joined": pltpu.make_async_copy(joined_w, w_one.at[pl.ds(0, width), pl.ds(0, jw)], load_sem.at[1]),
        "dense": pltpu.make_async_copy(dense_w, w_dense, load_sem.at[2]),
        "up": pltpu.make_async_copy(up_w, w_up, load_sem.at[3]),
        "down": pltpu.make_async_copy(down_w, w_one.at[pl.ds(0, hidden), pl.ds(0, width)], load_sem.at[4]),
        "adown": pltpu.make_async_copy(adown, tab_d.at[z], load_sem.at[5]),
        "aup": pltpu.make_async_copy(aup.at[:, :, half_cols], tab_u.at[z], load_sem.at[6]),
    }
    tabs, sel_outs, sel_ins = (tab_d, tab_u), (sel_out_d, sel_out_u), (sel_in_d, sel_in_u)

    def first_chip(t):
        return rem(y + div(t, own), chips)

    def request(chip, core, s):
        return chip * (2 * own) + core * own + s

    def tok_copy(t, h):
        q = request(first_chip(t), h, rem(t, own))
        return pltpu.make_async_copy(
            tokens.at[pl.ds(pl.multiple_of(q * slot, slot), slot)],
            tok.at[rem(t, 2), pl.ds(h * slot, slot)],
            tok_sem.at[rem(t, 2), h],
        )

    for h in range(2):
        tok_copy(0, h).start()
    loads["adown"].start()
    loads["aup"].start()
    loads["joined"].start()
    res_loads = []
    for chip in range(chips):
        for s in range(own):
            q = request(chip, c, s)
            res_loads.append(
                pltpu.make_async_copy(
                    tokens.at[pl.ds(pl.multiple_of(q * slot, slot), slot)],
                    res.at[chip * own + s],
                    res_sem.at[chip * own + s],
                )
            )

    barrier = pltpu.get_barrier_semaphore()
    for k in range(1, n_req):
        pl.semaphore_signal(barrier, inc=1, device_id=(lax.rem(r + k, n_req), m), device_id_type=MESH)
    for k in range(1, n_mlp):
        pl.semaphore_signal(barrier, inc=1, device_id=(r, peer(k)), device_id_type=MESH)

    key_at = (lax.broadcasted_iota(jnp.int32, (1, total), 1) - pre).astype(F32)
    mine = pl.ds(pl.multiple_of(c * slot, slot), slot)
    theirs = pl.ds(pl.multiple_of((1 - c) * slot, slot), slot)

    def norm_tokens(t):
        for h in range(2):
            tok_copy(t, h).wait()
        b = rem(t, 2)

        def one(i):
            at = pl.ds(pl.multiple_of(i * 64, 64), 64)
            tok[b, at] = layer_norm(tok[b, at].astype(F32), gain_one[...])

        loop(2 * slot // 64, one)

    def project(t):
        b = rem(t, 2)
        tile = jw // 2 if jw % 256 == 0 else jw

        def one(i):
            at = pl.ds(pl.multiple_of(i * tile, tile), tile)
            joined[b, :, at] = jnp.dot(
                tok[b], w_one[pl.ds(0, width), at], preferred_element_type=F32
            ).astype(BF16)

        loop(jw // tile, one)

    def keep(t, h):
        q = request(first_chip(t), h, rem(t, own))
        b = rem(t, 2)
        rows = pl.ds(pl.multiple_of(h * slot, slot), slot)
        valid = lax.broadcasted_iota(jnp.int32, (slot, 2 * HD), 0) < lens[q]
        for k in range(heads):
            at = k * 3 * HD + HD
            fresh[q, :, k * 2 * HD : (k + 1) * 2 * HD] = jnp.where(
                valid, joined[b, rows, at : at + 2 * HD], jnp.zeros((), BF16)
            )

    def attend(t, h):
        q = request(first_chip(t), h, rem(t, own))
        b = rem(t, 2)
        length = lens[q]
        g = groups[q]
        rows = pl.ds(pl.multiple_of(h * slot, slot), slot)
        own_row = lax.broadcasted_iota(jnp.int32, (slot, slot), 0)
        own_col = lax.broadcasted_iota(jnp.int32, (slot, slot), 1)
        allowed = (own_col <= own_row) & (own_col < length)
        pages = [table[g, p] for p in range(n_pages)]
        values, scores, mixed = [], [], []
        for k in range(heads):
            at = k * 3 * HD
            query = joined[b, rows, at : at + HD]
            kv = joined[b, rows, at + HD : at + 3 * HD]
            keys = jnp.concatenate(
                [pool_v[i, :, k * 2 * HD : k * 2 * HD + HD] for i in pages] + [kv[:, :HD]], axis=0
            )
            values.append(
                jnp.concatenate(
                    [pool_v[i, :, k * 2 * HD + HD : (k + 1) * 2 * HD] for i in pages] + [kv[:, HD:]], axis=0
                )
            )
            scores.append(
                lax.dot_general(query, keys, (((1,), (1,)), ((), ())), preferred_element_type=F32)
            )
        for k in range(heads):
            slope = jnp.float32(0.0)
            for i in range(n_mlp):
                here = 2.0 ** (-8.0 * (i * heads + k + 1.0) / HEADS) * LOG2E
                slope = jnp.where(m == i, jnp.float32(here), slope)
            score = scores[k] * (LOG2E / math.sqrt(HD)) + slope * key_at
            score = jnp.concatenate(
                [score[:, :pre], jnp.where(allowed, score[:, pre:], -jnp.inf)], axis=1
            )
            top = jnp.max(score, axis=-1, keepdims=True)
            weights = jnp.exp2(score - top)
            inverse = 1.0 / jnp.sum(weights, axis=-1, keepdims=True)
            weights = (weights * inverse).astype(BF16)
            mixed.append(jnp.dot(weights, values[k], preferred_element_type=F32))
        for k in range(heads):
            att[t, rows, k * HD : (k + 1) * HD] = mixed[k].astype(BF16)

    def part_copy(t):
        b = rem(t, 2)
        return remote(part.at[b, theirs], feed_in.at[t], part_s.at[t], part_r.at[t], r, partner)

    def dense(t):
        b = rem(t, 2)
        tile = min(1024, width)

        def one(i):
            at = pl.ds(pl.multiple_of(i * tile, tile), tile)
            part[b, :, at] = jnp.dot(att[t], w_dense[:, at], preferred_element_type=F32).astype(BF16)

        loop(width // tile, one)

    def pair_copy(t, jy, p):
        at = first_chip(t) * own + rem(t, own)
        on = pl.ds(p * (slot // 2), slot // 2)
        return remote(
            pair_own.at[at, on],
            pair_in.at[jy - 1, at, on],
            pair_s.at[t, jy - 1, p],
            pair_r.at[jy - 1, at, p],
            r,
            peer(2 * jy),
        )

    def pair_arrive(jy, at, p):
        on = pl.ds(p * (slot // 2), slot // 2)
        return remote(
            pair_own.at[at, on],
            pair_in.at[jy - 1, at, on],
            pair_s.at[0, jy - 1, p],
            pair_r.at[jy - 1, at, p],
            r,
            partner,
        )

    def pair_send(t, p):
        for jy in range(1, chips):
            pair_copy(t, jy, p).start()

    def pair(t):
        part_copy(t).wait_recv()
        b = rem(t, 2)
        at = first_chip(t) * own + rem(t, own)

        def one(i):
            on = pl.ds(i, 16)
            from_mine = pl.ds(pl.multiple_of(c * slot + i, 16), 16)
            pair_own[at, on] = (part[b, from_mine].astype(F32) + feed_in[t, on].astype(F32)).astype(BF16)

        blocks(slot, one)
        pair_send(t, 0)

    def line_up(kind, step):
        at = jnp.maximum(z - step, 0)
        return (z + 1 < lines) & (z - step >= 0), remote(
            tabs[kind].at[at],
            tabs[kind].at[at],
            tab_s.at[kind, 0, step],
            tab_r.at[kind, at],
            jnp.minimum(r + chips, n_req - 1),
            m,
        )

    def line_down(kind, step):
        at = jnp.minimum(z + step, lines - 1)
        return (z - 1 >= 0) & (z + step < lines), remote(
            tabs[kind].at[at],
            tabs[kind].at[at],
            tab_s.at[kind, 1, step],
            tab_r.at[kind, at],
            jnp.maximum(r - chips, 0),
            m,
        )

    def line_arrive(kind, at):
        return remote(tabs[kind].at[at], tabs[kind].at[at], tab_s.at[kind, 0, 0], tab_r.at[kind, at], r, m)

    def line_step(kind, step):
        if step > 0:
            @pl.when(z - step >= 0)
            def _():
                line_arrive(kind, jnp.maximum(z - step, 0)).wait_recv()

            @pl.when(z + step < lines)
            def _():
                line_arrive(kind, jnp.minimum(z + step, lines - 1)).wait_recv()

        if step < lines - 1:
            for go, copy in (line_up(kind, step), line_down(kind, step)):
                @pl.when(go)
                def _(copy=copy):
                    copy.start()

    def line_point(kind, place):
        for step in range(1, lines):
            if min(step, 3) == place:
                line_step(kind, step)

    def line_end():
        for kind in range(2):
            for step in range(lines - 1):
                for go, copy in (line_up(kind, step), line_down(kind, step)):
                    @pl.when(go)
                    def _(copy=copy):
                        copy.wait_send()

    def table_row(request_index):
        return id_rows[ids[request_index]]

    def sel_copy(kind, jx):
        to = z * chips + lax.rem(x + jx, chips)
        return remote(
            sel_outs[kind].at[jx - 1],
            sel_ins[kind].at[jx - 1],
            sel_s.at[kind, jx - 1],
            sel_r.at[kind, jx - 1],
            to,
            m,
        )

    def select_send(kind):
        for jx in range(1, chips):
            to = z * chips + lax.rem(x + jx, chips)

            def one(q):
                t = table_row(to * nq + q)
                sel_outs[kind][jx - 1, q] = tabs[kind][div(t, rows_per * chips), rem(t, rows_per)]

            loop(nq, one)
            sel_copy(kind, jx).start()

    def select_take(kind):
        for jx in range(1, chips):
            sel_copy(kind, jx).wait_recv()

        def one(q):
            t = table_row(r * nq + q)
            o = div(t, rows_per)
            jx = rem(x - rem(o, chips) + chips, chips)
            here = tabs[kind][div(o, chips), rem(t, rows_per)]
            there = sel_ins[kind][jnp.maximum(jx - 1, 0), q]
            both = jnp.where(jx == 0, here, there)
            if kind == 0:
                down_rows[q] = both
            else:
                chip, left = div(q, 2 * own), rem(q, 2 * own)
                up_out[div(left, own), chip * own + rem(left, own)] = both

        loop(nq, one)
        if kind == 1:
            uprow_copy().start()
            up_rows[:, :, half_cols] = up_out[c]

    def uprow_copy():
        return remote(up_out.at[1 - c], up_rows.at[:, :, half_cols], uprow_s.at[0], uprow_r.at[0], r, partner)

    def low_copy(jj):
        h = lax.rem(c + jj, 2)
        return remote(low_out.at[h], low_in.at[jj - 1], low_s.at[jj - 1], low_r.at[jj - 1], r, peer(jj))

    def low_parts():
        def one(i):
            t, h = div(i, 2), rem(i, 2)
            chip = first_chip(t)
            q = request(chip, h, rem(t, own))
            low_out[h, chip * own + rem(t, own)] = lax.dot_general(
                down_rows[q],
                att[t, pl.ds(pl.multiple_of(h * slot, slot), slot)],
                (((1,), (1,)), ((), ())),
                preferred_element_type=F32,
            ).astype(BF16)

        loop(chunks * 2, one)
        for jj in range(1, n_mlp):
            low_copy(jj).start()

    def mig_copy(j):
        return remote(
            mig_out.at[j - 1], mig_in.at[j - 1], mig_s.at[j - 1], mig_r.at[j - 1], rem(r + j, n_req), m
        )

    def migrate(along):
        def one(i):
            j = i + 1

            @pl.when((rem(j, chips) == 0) == along)
            def _():
                to = rem(r + j, n_req)
                leaving = jnp.int32(0)
                for k in range(moves):
                    leaving = jnp.where(div(landing[r * moves + k], nq) == to, migrants[k], leaving)
                mig_out[j - 1] = fresh[leaving]
                mig_copy(j).start()

        loop(n_req - 1, one)

    def page_copy(s):
        return pltpu.make_async_copy(mig_out.at[s], page_out.at[s], page_sem.at[s])

    def merge():
        for j in range(1, n_req):
            mig_copy(j).wait()

        def one(s):
            def find(k, owner):
                return jnp.where(landing[k] == r * nq + s, div(k, moves), owner)

            owner = lax.fori_loop(0, n_req * moves, find, jnp.int32(-1), unroll=8)
            at = jnp.maximum(rem(r - owner + n_req, n_req) - 1, 0)
            mig_out[s] = jnp.where(owner >= 0, mig_in[at], fresh[s])
            page_copy(s).start()

        loop(nq, one)

    norm_tokens(0)
    pl.semaphore_wait(barrier, n_req - 1 + n_mlp - 1)
    loads["adown"].wait()
    loads["aup"].wait()
    line_step(1, 0)

    def phase_one(u):
        @pl.when(u < chunks)
        def _():
            t = u

            @pl.when(t > 0)
            def _():
                norm_tokens(t)

            @pl.when(t == 0)
            def _():
                loads["joined"].wait()
                loads["pool"].start()
                loads["dense"].start()
                for h in range(2):
                    if chunks > 1:
                        tok_copy(1, h).start()
                for d in res_loads:
                    d.start()
                loads["up"].start()

            project(t)

            @pl.when(t + 2 < chunks)
            def _():
                for h in range(2):
                    tok_copy(t + 2, h).start()

            @pl.when(t == 0)
            def _():
                line_step(0, 0)
                loads["pool"].wait()

            @pl.when(t == 1)
            def _():
                loop(2, lambda h: keep(0, h))

            @pl.when(t > 0)
            def _():
                loop(2, lambda h: keep(t, h))

            @pl.when(t == chunks - 1)
            def _():
                loads["down"].start()
                line_point(0, 3)
                select_send(0)
                migrate(True)

        @pl.when(u != 1)
        def _():
            t = u - (u > 1).astype(jnp.int32)
            loop(2, lambda h: attend(t, h))

            @pl.when(t == 0)
            def _():
                loads["dense"].wait()

            @pl.when(t >= 2)
            def _():
                part_copy(t - 2).wait_send()

            dense(t)
            part_copy(t).start()

            @pl.when(t == 0)
            def _():
                line_point(1, 1)

            @pl.when(t < 2)
            def _():
                pair(t)
                pair_send(t, 1)

        @pl.when(u == 1)
        def _():
            line_point(1, 2)
            line_point(0, 1)

        @pl.when(u == 2)
        def _():
            line_point(1, 3)
            select_send(1)
            line_point(0, 2)

    loop(chunks + 1, phase_one)
    pair(2)
    select_take(0)
    low_parts()
    pair_send(2, 1)
    for t in range(3, chunks):
        pair(t)
        pair_send(t, 1)
    select_take(1)
    migrate(False)
    uprow_copy().wait_recv()
    for jj in range(1, n_mlp):
        low_copy(jj).wait_recv()
    loads["up"].wait()
    loads["down"].wait()
    for d in res_loads:
        d.wait()

    others = chunks - own

    def second_chip(t):
        return rem(y + 1 + div(t, own), chips)

    def norm_copy(t):
        return remote(normed.at[t, mine], normed.at[t, mine], norm_s.at[t], norm_r.at[t], r, partner)

    def residual(t):
        at = second_chip(t) * own + rem(t, own)
        for jy in range(1, chips):
            for p in range(2):
                pair_arrive(jy, at, p).wait_recv()
        low = low_out[c, at].astype(F32)
        for jj in range(1, n_mlp):
            low = low + low_in[jj - 1, at].astype(F32)
        low = low.astype(BF16)
        tile = min(512, width)

        def add(i):
            on = pl.ds(pl.multiple_of(i * tile, tile), tile)
            value = res[at, :, on].astype(F32) + pair_own[at, :, on].astype(F32)
            for jy in range(1, chips):
                value = value + pair_in[jy - 1, at, :, on].astype(F32)
            value = value + lax.dot_general(
                low, up_rows[at, :, on], (((0,), (0,)), ((), ())), preferred_element_type=F32
            )
            res[at, :, on] = value.astype(BF16)

        loop(width // tile, add)

        def one(i):
            to = pl.ds(pl.multiple_of(c * slot + i * 64, 64), 64)
            on = pl.ds(pl.multiple_of(i * 64, 64), 64)
            normed[t, to] = layer_norm(res[at, on].astype(F32), gain_two[...])

        loop(slot // 64, one)
        norm_copy(t).start()

    def expand(t):
        norm_copy(t).wait_recv()
        tile = min(1024, hidden)

        def one(i):
            at = pl.ds(pl.multiple_of(i * tile, tile), tile)
            expanded[:, at] = gelu_tanh(
                jnp.dot(normed[t], w_up[:, at], preferred_element_type=F32)
            ).astype(BF16)

        loop(hidden // tile, one)

    def feed_copy(t):
        b = rem(t, 2)
        return remote(feed.at[b, theirs], feed_in.at[t], feed_s.at[t], feed_r.at[t], r, partner)

    def contract(t):
        b = rem(t, 2)
        tile = min(1024, width)

        def one(i):
            at = pl.ds(pl.multiple_of(i * tile, tile), tile)
            feed[b, :, at] = jnp.dot(
                expanded[...], w_one[pl.ds(0, hidden), at], preferred_element_type=F32
            ).astype(BF16)

        loop(width // tile, one)
        feed_copy(t).start()

    def final_copy(t, p):
        on = pl.ds(p * (slot // 2), slot // 2)
        return remote(
            pair_feed.at[t, on],
            final_in.at[div(t, own), rem(t, own), on],
            final_s.at[t, p],
            final_r.at[div(t, own), rem(t, own), p],
            r,
            rem(m + 2 + 2 * div(t, own), n_mlp),
        )

    def final_arrive(jy, s, p):
        on = pl.ds(pl.multiple_of(p * (slot // 2), 16), slot // 2)
        return remote(
            pair_feed.at[0, on],
            final_in.at[jy - 1, s, on],
            final_s.at[0, p],
            final_r.at[jy - 1, s, p],
            r,
            partner,
        )

    def gather(t):
        feed_copy(t).wait_recv()
        b = rem(t, 2)

        def one(i):
            on = pl.ds(i, 16)
            from_mine = pl.ds(pl.multiple_of(c * slot + i, 16), 16)
            pair_feed[t, on] = (feed[b, from_mine].astype(F32) + feed_in[t, on].astype(F32)).astype(BF16)

        blocks(slot, one)
        for p in range(2):
            final_copy(t, p).start()

    def phase_two(u):
        @pl.when(u < chunks)
        def _():
            residual(u)

        @pl.when(u > 0)
        def _():
            t = u - 1
            expand(t)

            @pl.when(t >= 2)
            def _():
                feed_copy(t - 2).wait_send()

            contract(t)

            @pl.when(t < others)
            def _():
                gather(t)

    loop(chunks + 1, phase_two)
    for t in range(max(chunks - 2, 0), chunks):
        part_copy(t).wait_send()
    for t in range(chunks):
        for jy in range(1, chips):
            for p in range(2):
                pair_copy(t, jy, p).wait_send()
        norm_copy(t).wait_send()
    line_end()
    for kind in range(2):
        for jx in range(1, chips):
            sel_copy(kind, jx).wait_send()
    uprow_copy().wait_send()
    for jj in range(1, n_mlp):
        low_copy(jj).wait_send()
    merge()

    def out_copy(s, p):
        on = pl.ds(pl.multiple_of(p * (slot // 2), 16), slot // 2)
        to = pl.ds(pl.multiple_of(s * slot + p * (slot // 2), 16), slot // 2)
        return pltpu.make_async_copy(out_v.at[s, on], layer_out.at[to], out_sem.at[s, p])

    def finish(k):
        s, p = div(k, 2), rem(k, 2)
        t = others + s
        b = rem(t, 2)
        at = y * own + s

        @pl.when(p == 0)
        def _():
            feed_copy(t).wait_recv()

        for jy in range(1, chips):
            final_arrive(jy, s, p).wait_recv()
        length = lens[m * own + s]

        def one(i):
            row = p * (slot // 2) + i
            on = pl.ds(pl.multiple_of(row, 16), 16)
            from_mine = pl.ds(pl.multiple_of(c * slot + row, 16), 16)
            value = res[at, on].astype(F32) + (feed[b, from_mine].astype(F32) + feed_in[t, on].astype(F32))
            for jy in range(1, chips):
                value = value + final_in[jy - 1, s, on].astype(F32)
            valid = lax.broadcasted_iota(jnp.int32, (16, width), 0) + row < length
            out_v[s, on] = jnp.where(valid, value, 0.0).astype(BF16)

        blocks(slot // 2, one)
        out_copy(s, p).start()

    loop(own * 2, finish)
    for t in range(others):
        for p in range(2):
            final_copy(t, p).wait_send()
    for t in range(max(chunks - 2, 0), chunks):
        feed_copy(t).wait_send()
    for s in range(own):
        for p in range(2):
            out_copy(s, p).wait()
    for s in range(nq):
        page_copy(s).wait()


def copy_body(first_in, second_in, first_out, second_out, first_v, second_v, sems):
    comes, goes = [], []
    for src, mid, dst in ((first_in, first_v, first_out), (second_in, second_v, second_out)):
        rows = src.shape[0] // 4
        for i in range(4):
            at = pl.ds(i * rows, rows)
            comes.append(pltpu.make_async_copy(src.at[at], mid.at[at], sems.at[0, len(comes)]))
            goes.append(pltpu.make_async_copy(mid.at[at], dst.at[at], sems.at[1, len(goes)]))
    for d in comes:
        d.start()
    for come, go in zip(comes, goes):
        come.wait()
        go.start()
    for d in goes:
        d.wait()


def copy_out(first, second):
    hbm = pl.BlockSpec(memory_space=pl.ANY)
    return pl.pallas_call(
        copy_body,
        out_shape=(
            jax.ShapeDtypeStruct(first.shape, first.dtype),
            jax.ShapeDtypeStruct(second.shape, second.dtype),
        ),
        in_specs=[hbm, hbm],
        out_specs=(hbm, hbm),
        scratch_shapes=[
            pltpu.VMEM(first.shape, first.dtype),
            pltpu.VMEM(second.shape, second.dtype),
            pltpu.SemaphoreType.DMA((2, 8)),
        ],
        compiler_params=pltpu.CompilerParams(vmem_limit_bytes=60 * 1024 * 1024),
    )(first, second)


def shards(n_req, n_mlp, *args):
    (
        tokens,
        first_gain,
        joined_weight,
        dense_weight,
        adapter_down,
        adapter_up,
        adapter_ids,
        adapter_rows,
        second_gain,
        up_weight,
        down_weight,
        page_pool,
        page_table,
        group_index,
        lengths,
        migrants,
        landing,
    ) = args
    chips = n_mlp // 2
    lines = n_req // chips
    nq = lengths.shape[0]
    slot = tokens.shape[0] // nq
    width = tokens.shape[1]
    jw = joined_weight.shape[1]
    heads = jw // (3 * HD)
    cols = heads * HD
    own = nq // n_mlp
    chunks = chips * own
    hidden = up_weight.shape[1]
    rank = adapter_down.shape[1]
    kv = page_pool.shape[2]
    dma = pltpu.SemaphoreType.DMA
    vm = pltpu.VMEM
    others = max(chips - 1, 1)
    scratch = [
        vm((max(width, hidden), max(jw, width)), BF16),
        vm((width, hidden), BF16),
        vm(dense_weight.shape, BF16),
        vm(page_pool.shape, BF16),
        vm((2, 2 * slot, width), BF16),
        vm((2, 2 * slot, jw), BF16),
        vm((chunks, 2 * slot, cols), BF16),
        vm((2, 2 * slot, width), BF16),
        vm((chunks, slot, width), BF16),
        vm((others, chunks, slot, width), BF16),
        vm((nq, slot, kv), BF16),
        vm((max(nq, n_req - 1), slot, kv), BF16),
        vm((n_req - 1, slot, kv), BF16),
        vm((chunks, slot, width), BF16),
        vm((chunks, 2 * slot, width), BF16),
        vm((2 * slot, hidden), BF16),
        vm((2, 2 * slot, width), BF16),
        vm((chunks, slot, width), BF16),
        vm((max(chunks - own, 1), slot, width), BF16),
        vm((others, own, slot, width), BF16),
        vm((own, slot, width), BF16),
        vm((lines, adapter_down.shape[0], rank, cols), BF16),
        vm((others, nq, rank, cols), BF16),
        vm((others, nq, rank, cols), BF16),
        vm((lines, adapter_down.shape[0], rank, width // 2), BF16),
        vm((others, nq, rank, width // 2), BF16),
        vm((others, nq, rank, width // 2), BF16),
        vm((nq, rank, cols), BF16),
        vm((2, chunks, rank, width // 2), BF16),
        vm((chunks, rank, width), BF16),
        vm((2, chunks, rank, slot), BF16),
        vm((n_mlp - 1, chunks, rank, slot), BF16),
        dma((7,)),
        dma((2, 2)),
        dma((chunks,)),
        dma((own, 2)),
        dma((nq,)),
        dma((chunks,)),
        dma((chunks,)),
        dma((chunks, others, 2)),
        dma((others, chunks, 2)),
        dma((n_req - 1,)),
        dma((n_req - 1,)),
        dma((chunks,)),
        dma((chunks,)),
        dma((chunks,)),
        dma((chunks,)),
        dma((chunks, 2)),
        dma((others, own, 2)),
        dma((2, 2, lines)),
        dma((2, lines)),
        dma((2, others)),
        dma((2, others)),
        dma((1,)),
        dma((1,)),
        dma((n_mlp - 1,)),
        dma((n_mlp - 1,)),
    ]
    smem = pl.BlockSpec(memory_space=pltpu.SMEM)
    vmem = pl.BlockSpec(memory_space=pltpu.VMEM)
    hbm = pl.BlockSpec(memory_space=pl.ANY)
    rows, pages = pl.pallas_call(
        functools.partial(body, n_req, n_mlp),
        out_shape=(
            jax.ShapeDtypeStruct((own * slot, width), BF16),
            jax.ShapeDtypeStruct((nq, slot, kv), BF16),
        ),
        in_specs=[smem] * 7 + [vmem] * 2 + [hbm] * 8,
        out_specs=(hbm, hbm),
        scratch_shapes=scratch,
        compiler_params=pltpu.CompilerParams(
            collective_id=0, has_side_effects=True, vmem_limit_bytes=63 * 1024 * 1024
        ),
    )(
        adapter_ids,
        adapter_rows,
        page_table,
        group_index,
        lengths,
        migrants,
        landing,
        first_gain.reshape(1, -1),
        second_gain.reshape(1, -1),
        tokens,
        joined_weight,
        dense_weight,
        adapter_down,
        adapter_up,
        up_weight,
        down_weight,
        page_pool,
    )
    return copy_out(rows, pages)


def solution(mesh):
    return jax.shard_map(
        functools.partial(shards, mesh.shape["req"], mesh.shape["mlp"]),
        mesh=mesh,
        in_specs=(
            P("req", None),
            P(),
            P(None, "mlp"),
            P("mlp", None),
            P("req", None, "mlp"),
            P("req", None, None),
            P(),
            P(),
            P(),
            P(None, "mlp"),
            P("mlp", None),
            P("req", None, "mlp"),
            P("req", None),
            P("req"),
            P("req"),
            P("req"),
            P(),
        ),
        out_specs=(P(("req", "mlp"), None), P("req", None, "mlp")),
        check_vma=False,
    )
```
